256 devices in a mesh: tm: 8 (over z), height: 16 (over x, y), cam: 2 (over core).
Axes of the slice: x: 4, y: 4, z: 8, core: 2. Of those that a mesh axis runs over, the one named last changes fastest.
Arguments:
- video_clip: bfloat16 [2, 32, 128, 64, 256], P('cam', 'tm', 'height'), may hold values from -6 to 6
- valid_from: int32 [2], P('cam'), may hold values from 0 to 16, as said below
- norm_gain: float32 [256], replicated, may hold values from 0.5 to 1.5
- spatial_weight: bfloat16 [3, 3, 256, 256], replicated, may hold values from -0.125 to 0.125
- temporal_weight: bfloat16 [3, 256, 256], replicated, may hold values from -0.21875 to 0.21875
- mix_weight: bfloat16 [3, 256, 256], replicated, may hold values from -0.21875 to 0.21875
- cotangent: bfloat16 [2, 16, 128, 64, 256], P('cam', None, ('height', 'tm')), may hold values from -6 to 6
Outputs:
- encoded: bfloat16 [2, 16, 128, 64, 256], P('cam', None, ('height', 'tm'))
- video_gradient: bfloat16 [2, 32, 128, 64, 256], P('cam', 'tm', 'height')
- spatial_gradient: float32 [3, 3, 256, 256], replicated
- temporal_gradient: float32 [3, 256, 256], replicated
- mix_gradient: float32 [3, 256, 256], replicated
- gain_gradient: float32 [256], replicated
The draws below stay inside these ranges and needn't reach their ends.
Inputs may be any that keep to these rules, and one draw needn't show every extreme that they name: Frames before valid_from of a camera are padding. In every draw some camera starts at 16.
All inputs are finite; a program needn't handle non-finite values.
Results may differ from the reference program's by a relative error of at most 0.0065.
Values may be sent and summed in bfloat16 or wider, within the bound.
A program may use at most 128 MiB of HBM per device.

```python
import math
import jax
import jax.numpy as jnp
from jax import lax

C = 256
W = 64
CAMS = 2
T_IN = 32
T_OUT = 16
H = 128


def draw_valid_from(key, part):
    starts = jax.random.randint(jax.random.fold_in(key, 11), (CAMS,), 0, T_IN // 2)
    latest = jax.random.randint(jax.random.fold_in(key, 12), (), 0, CAMS)
    starts = starts.at[latest].set(T_IN // 2)
    return starts.astype(jnp.int32)


def block_scale(key, extent, cuts, least, top_value):
    gain = 1.0
    for axis_at, shards_of in cuts:
        heights = jax.random.uniform(jax.random.fold_in(jax.random.fold_in(key, 6), axis_at), (shards_of,), jnp.float32, least / len(cuts), top_value / len(cuts))
        gain = gain * jnp.repeat(jnp.exp(heights), extent[axis_at] // shards_of).reshape((-1,) + (1,) * (len(extent) - 1 - axis_at))
    return gain


def scatter_about(rng, shape, width, limit, pieces=(), held_as=jnp.bfloat16):
    entries = width * jax.random.normal(rng, shape, jnp.float32)
    if pieces:
        entries = entries * block_scale(rng, shape, pieces, -0.22, 0.18)
    return jnp.clip(entries, -limit, limit).astype(held_as)


def setup_inputs(seed: int = 0) -> dict:
    key_of = jax.random.split(jax.random.key(seed), 8)
    video_clip = scatter_about(key_of[0], (CAMS, T_IN, H, W, C), 1.0, 6.0, ((0, 2), (1, 8), (2, 16)))
    valid_from = draw_valid_from(jax.random.fold_in(key_of[7], 71), 0)
    norm_gain = jnp.clip(1.0 + 0.1 * jax.random.normal(key_of[2], (C,), jnp.float32), 0.5, 1.5)
    spatial_weight = scatter_about(key_of[3], (3, 3, C, C), (9 * C) ** -0.5, 0.125)
    temporal_weight = scatter_about(key_of[4], (3, C, C), (3 * C) ** -0.5, 0.21875)
    mix_weight = scatter_about(key_of[5], (3, C, C), (3 * C) ** -0.5, 0.21875)
    cotangent = scatter_about(key_of[6], (CAMS, T_OUT, H, W, C), 1.0, 6.0, ((0, 2), (2, 128)))
    return dict(video_clip=video_clip, valid_from=valid_from, norm_gain=norm_gain, spatial_weight=spatial_weight, temporal_weight=temporal_weight, mix_weight=mix_weight, cotangent=cotangent)


def project(rows_in, weight):
    flat_rows = rows_in.reshape(-1, rows_in.shape[-1])
    product = jnp.dot(flat_rows, weight, preferred_element_type=jnp.float32)
    return product.reshape(rows_in.shape[:-1] + (weight.shape[-1],))

def project_back(rows_in, weight):
    flat_rows = rows_in.reshape(-1, rows_in.shape[-1])
    product = lax.dot_general(flat_rows, weight, (((1,), (1,)), ((), ())), preferred_element_type=jnp.float32)
    return product.reshape(rows_in.shape[:-1] + (weight.shape[0],))

def outer_sum(left_rows, right_rows):
    return lax.dot_general(left_rows.reshape(-1, left_rows.shape[-1]), right_rows.reshape(-1, right_rows.shape[-1]), (((0,), (0,)), ((), ())), preferred_element_type=jnp.float32)

def column_pad(padded):
    return jnp.pad(padded, ((0, 0), (0, 0), (0, 0), (1, 1), (0, 0)))

def spatial(padded, weight):
    columns = column_pad(padded)
    rows_here = padded.shape[2] - 2
    width_here = padded.shape[3]
    accumulated = jnp.zeros(padded.shape[:2] + (rows_here, width_here, weight.shape[-1]), jnp.float32)
    for row_tap in range(3):
        for column_tap in range(3):
            window = columns[:, :, row_tap:row_tap + rows_here, column_tap:column_tap + width_here]
            accumulated = accumulated + project(window, weight[row_tap, column_tap])
    return accumulated

def spatial_grad(padded, gradient):
    columns = column_pad(padded)
    rows_here = padded.shape[2] - 2
    width_here = padded.shape[3]
    outer_rows = []
    for row_tap in range(3):
        inner_rows = []
        for column_tap in range(3):
            window = columns[:, :, row_tap:row_tap + rows_here, column_tap:column_tap + width_here]
            inner_rows.append(outer_sum(window, gradient))
        outer_rows.append(jnp.stack(inner_rows))
    return jnp.stack(outer_rows)

def flipped(weight):
    return jnp.transpose(weight[::-1, ::-1], (0, 1, 3, 2))

def norm_forward(masked, norm_gain):
    values = masked.astype(jnp.float32)
    inverse = lax.rsqrt(lax.optimization_barrier(jnp.mean(values * values, axis=-1, keepdims=True)) + 1e-06)
    unit_rows = values * inverse
    return ((unit_rows * norm_gain).astype(jnp.bfloat16), unit_rows, inverse)

def norm_backward(normed_gradient, unit_rows, inverse, norm_gain, present):
    unit_gradient = normed_gradient * norm_gain
    masked_gradient = inverse * (unit_gradient - unit_rows * lax.optimization_barrier(jnp.mean(unit_gradient * unit_rows, axis=-1, keepdims=True)))
    video_gradient = jnp.where(present, masked_gradient, jnp.zeros_like(masked_gradient)).astype(jnp.bfloat16)
    gain_gradient = lax.optimization_barrier(jnp.sum((normed_gradient * unit_rows).reshape(-1, unit_rows.shape[-1]), axis=0))
    return (video_gradient, gain_gradient)

def split_frames(active, prior_frame):
    dims_in = active.shape
    frame_pairs = active.reshape(dims_in[0], dims_in[1] // 2, 2, dims_in[2], dims_in[3], dims_in[4])
    even_frames = frame_pairs[:, :, 0]
    odd_frames = frame_pairs[:, :, 1]
    prior_odd = jnp.concatenate([prior_frame, odd_frames[:, :-1]], axis=1)
    return (even_frames, odd_frames, prior_odd)

def temporal_forward(even_frames, odd_frames, prior_odd, weight):
    accumulated = project(odd_frames, weight[0]) + project(even_frames, weight[1]) + project(prior_odd, weight[2])
    return accumulated.astype(jnp.bfloat16)

def temporal_backward(even_frames, odd_frames, prior_odd, strided_gradient, following, weight):
    weight_gradient = jnp.stack([outer_sum(odd_frames, strided_gradient), outer_sum(even_frames, strided_gradient), outer_sum(prior_odd, strided_gradient)])
    next_gradient = jnp.concatenate([strided_gradient[:, 1:], following], axis=1)
    odd_gradient = project_back(strided_gradient, weight[0]) + project_back(next_gradient, weight[2])
    even_gradient = project_back(strided_gradient, weight[1])
    dims_in = even_frames.shape
    active_gradient = jnp.stack([even_gradient, odd_gradient], axis=2).reshape(dims_in[0], dims_in[1] * 2, dims_in[2], dims_in[3], dims_in[4])
    return (active_gradient, weight_gradient)

def mix_forward(regrouped, weight):
    frame_count = regrouped.shape[1]
    blank_frames = jnp.zeros(regrouped.shape[:1] + (2,) + regrouped.shape[2:], regrouped.dtype)
    history = jnp.concatenate([blank_frames, regrouped], axis=1)
    accumulated = regrouped.astype(jnp.float32)
    for offset in range(3):
        accumulated = accumulated + project(history[:, 2 - offset:2 - offset + frame_count], weight[offset])
    return (accumulated.astype(jnp.bfloat16), history)

def mix_backward(history, cotangent, weight):
    frame_count = cotangent.shape[1]
    mix_gradient = jnp.stack([outer_sum(history[:, 2 - offset:2 - offset + frame_count], cotangent) for offset in range(3)])
    blank_frames = jnp.zeros(cotangent.shape[:1] + (2,) + cotangent.shape[2:], cotangent.dtype)
    ahead = jnp.concatenate([cotangent, blank_frames], axis=1)
    accumulated = cotangent.astype(jnp.float32)
    for offset in range(3):
        accumulated = accumulated + project_back(ahead[:, offset:offset + frame_count], weight[offset])
    return (mix_gradient, accumulated.astype(jnp.bfloat16))

def activation_backward(active_gradient, pre_activation):
    sigmoid_value = jax.nn.sigmoid(pre_activation)
    return (active_gradient * sigmoid_value * (1.0 + pre_activation * (1.0 - sigmoid_value))).astype(jnp.bfloat16)

def reference(video_clip, valid_from, norm_gain, spatial_weight, temporal_weight, mix_weight, cotangent):
    frames = jnp.arange(T_IN, dtype=jnp.int32)
    present = (frames[None, :] >= valid_from[:, None])[:, :, None, None, None]
    masked = jnp.where(present, video_clip, jnp.zeros_like(video_clip))
    normed, unit_rows, inverse = norm_forward(masked, norm_gain)
    padded = jnp.pad(normed, ((0, 0), (0, 0), (1, 1), (0, 0), (0, 0)))
    pre_activation = spatial(padded, spatial_weight)
    active = jax.nn.silu(pre_activation).astype(jnp.bfloat16)
    prior_frame = jnp.zeros_like(active[:, :1])
    even_frames, odd_frames, prior_odd = split_frames(active, prior_frame)
    strided = temporal_forward(even_frames, odd_frames, prior_odd, temporal_weight)
    encoded, history = mix_forward(strided, mix_weight)
    mix_gradient, strided_gradient = mix_backward(history, cotangent, mix_weight)
    following = jnp.zeros_like(strided_gradient[:, :1])
    active_gradient, temporal_gradient = temporal_backward(even_frames, odd_frames, prior_odd, strided_gradient, following, temporal_weight)
    pre_gradient = activation_backward(active_gradient, pre_activation)
    spatial_gradient = spatial_grad(padded, pre_gradient)
    gradient_padded = jnp.pad(pre_gradient, ((0, 0), (0, 0), (1, 1), (0, 0), (0, 0)))
    normed_gradient = spatial(gradient_padded, flipped(spatial_weight))
    video_gradient, gain_gradient = norm_backward(normed_gradient, unit_rows, inverse, norm_gain, present)
    gradient_scale = 1.0 / math.sqrt(CAMS * T_IN * H * W)
    return (encoded, video_gradient, spatial_gradient * gradient_scale, temporal_gradient * gradient_scale, mix_gradient * gradient_scale, gain_gradient * gradient_scale)
```

```python
import functools
import math

import jax
import jax.numpy as jnp
from jax import lax
from jax.experimental import pallas as pl
from jax.experimental.pallas import tpu as pltpu
from jax.sharding import PartitionSpec as P

MESH = pl.DeviceIdType.MESH
BF = jnp.bfloat16
F32 = jnp.float32
LARGE = 12 * 256
SMALL = 4 * 256
VMEM_LIMIT = 46 << 20


class Place:
    def __init__(self):
        self.z = lax.axis_index("tm")
        self.h = lax.axis_index("height")
        self.c = lax.axis_index("cam")
        self.x = self.h // 4
        self.y = self.h % 4
        self.first = (1 - self.c) * self.x + self.c * self.y
        self.second = (1 - self.c) * self.y + self.c * self.x

    def across(self):
        return {"cam": 1 - self.c}

    def along_first(self, d):
        other = (self.first + d) % 4
        return {"height": (1 - self.c) * (other * 4 + self.y) + self.c * (self.x * 4 + other)}

    def along_second(self, d):
        other = (self.second + d) % 4
        return {"height": (1 - self.c) * (self.x * 4 + other) + self.c * (other * 4 + self.y)}

    def along_z(self, d):
        return {"tm": (self.z + d) % 8}


def remote(src, dst, send, recv, where):
    return pltpu.make_async_remote_copy(
        src_ref=src, dst_ref=dst, send_sem=send, recv_sem=recv, device_id=where, device_id_type=MESH
    )


def greet(peers):
    barrier = pltpu.get_barrier_semaphore()
    for peer in peers:
        pl.semaphore_signal(barrier, inc=1, device_id=peer, device_id_type=MESH)
    return barrier, len(peers)


def reduce_peers(place):
    return (
        [place.across()]
        + [place.along_first(d) for d in (1, 2, 3)]
        + [place.along_second(d) for d in (1, 2, 3)]
        + [place.along_z(d) for d in range(1, 8)]
    )


def block(ref, start, rows):
    return ref.at[pl.ds(pl.multiple_of(start, 16), rows)]


def started(copies):
    for copy in copies:
        copy.start()
    return copies


def finished(copies):
    for copy in copies:
        copy.wait()


class DeviceSum:
    def __init__(self, place, total, base, gathered, scratch):
        self.place, self.total, self.base, self.gathered = place, total, base, gathered
        (
            self.halved,
            self.landed_c,
            self.held_1,
            self.landed_1,
            self.held_2,
            self.landed_2,
            self.held_3,
            self.landed_3,
            self.placed_3,
        ) = scratch[:9]
        self.sems = scratch[9:]
        rows = gathered.shape[0]
        self.half, self.n1, self.n2, self.n3 = rows // 2, rows // 8, rows // 32, rows // 256
        self.mine = place.c * self.half
        self.at_1 = self.mine + place.first * self.n1
        self.at_2 = self.at_1 + place.second * self.n2

    def start_core(self):
        other = pl.multiple_of(self.base + (1 - self.place.c) * self.half, 16)
        self.halved[...] = self.total[pl.ds(other, self.half), :].astype(BF)
        s, r = self.sems[0], self.sems[1]
        self.pending = started([remote(self.halved, self.landed_c, s, r, self.place.across())])

    def start_first(self):
        finished(self.pending)
        own = pl.multiple_of(self.base + self.mine, 16)
        self.held_1[...] = (self.total[pl.ds(own, self.half), :] + self.landed_c[...].astype(F32)).astype(BF)
        s, r = self.sems[2], self.sems[3]
        self.pending = started(
            [
                remote(
                    block(self.held_1, (self.place.first + d) % 4 * self.n1, self.n1),
                    self.landed_1.at[d - 1],
                    s.at[d - 1],
                    r.at[d - 1],
                    self.place.along_first(d),
                )
                for d in (2, 1, 3)
            ]
        )

    def start_second(self):
        finished(self.pending)
        sum_here = self.held_1[pl.ds(pl.multiple_of(self.place.first * self.n1, 16), self.n1), :].astype(F32)
        for k in range(3):
            sum_here = sum_here + self.landed_1[k].astype(F32)
        self.held_2[...] = sum_here.astype(BF)
        s, r = self.sems[4], self.sems[5]
        self.pending = started(
            [
                remote(
                    block(self.held_2, (self.place.second + d) % 4 * self.n2, self.n2),
                    self.landed_2.at[d - 1],
                    s.at[d - 1],
                    r.at[d - 1],
                    self.place.along_second(d),
                )
                for d in (2, 1, 3)
            ]
        )

    def second_sum(self):
        finished(self.pending)
        sum_here = self.held_2[pl.ds(pl.multiple_of(self.place.second * self.n2, 16), self.n2), :].astype(F32)
        for k in range(3):
            sum_here = sum_here + self.landed_2[k].astype(F32)
        return sum_here

    def start_z(self):
        sum_here = self.second_sum()
        for k in range(8):
            self.held_3[k, 0 : self.n3] = sum_here[k * self.n3 : (k + 1) * self.n3].astype(BF)
        s, r = self.sems[6], self.sems[7]
        self.pending = started(
            [
                remote(
                    self.held_3.at[(self.place.z + d) % 8],
                    self.landed_3.at[d],
                    s.at[d],
                    r.at[d],
                    self.place.along_z(d),
                )
                for d in (4, 3, 5, 2, 6, 1, 7)
            ]
        )

    def start_z_back(self):
        finished(self.pending)
        z = self.place.z
        sum_here = self.held_3[z].astype(F32)
        for d in range(1, 8):
            sum_here = sum_here + self.landed_3[d].astype(F32)
        self.placed_3[z] = sum_here.astype(BF)
        s, r = self.sems[8], self.sems[9]
        self.pending = started(
            [
                remote(self.placed_3.at[z], self.placed_3.at[z], s.at[d], r.at[d], self.place.along_z(d))
                for d in (4, 3, 5, 2, 6, 1, 7)
            ]
        )

    def finish_z_back(self):
        finished(self.pending)
        pieces = [self.placed_3[k].astype(F32)[0 : self.n3] for k in range(8)]
        self.gathered[pl.ds(pl.multiple_of(self.at_2, 16), self.n2), :] = jnp.concatenate(pieces).astype(BF)

    def start_z_at_once(self):
        z = self.place.z
        self.landed_3[z] = self.second_sum().astype(BF)
        s, r = self.sems[6], self.sems[7]
        self.pending = started(
            [
                remote(self.landed_3.at[z], self.landed_3.at[z], s.at[d], r.at[d], self.place.along_z(d))
                for d in (4, 3, 5, 2, 6, 1, 7)
            ]
        )

    def finish_z_at_once(self):
        finished(self.pending)
        sum_here = self.landed_3[0].astype(F32)
        for k in range(1, 8):
            sum_here = sum_here + self.landed_3[k].astype(F32)
        self.gathered[pl.ds(pl.multiple_of(self.at_2, 16), self.n2), :] = sum_here.astype(BF)

    def start_second_back(self):
        at = block(self.gathered, self.at_2, self.n2)
        s, r = self.sems[10], self.sems[11]
        self.pending = started(
            [remote(at, at, s.at[d - 1], r.at[d - 1], self.place.along_second(d)) for d in (2, 1, 3)]
        )

    def start_first_back(self):
        finished(self.pending)
        at = block(self.gathered, self.at_1, self.n1)
        s, r = self.sems[12], self.sems[13]
        self.pending = started(
            [remote(at, at, s.at[d - 1], r.at[d - 1], self.place.along_first(d)) for d in (2, 1, 3)]
        )

    def start_core_back(self):
        finished(self.pending)
        at = block(self.gathered, self.mine, self.half)
        self.pending = started([remote(at, at, self.sems[14], self.sems[15], self.place.across())])

    def finish(self):
        finished(self.pending)


def sum_scratch(rows, at_once):
    dma, vmem = pltpu.SemaphoreType.DMA, pltpu.VMEM
    piece = rows // 32 if at_once else -(-rows // 256 // 16) * 16
    return [
        vmem((rows // 2, 256), BF),
        vmem((rows // 2, 256), BF),
        vmem((rows // 2, 256), BF),
        vmem((3, rows // 8, 256), BF),
        vmem((rows // 8, 256), BF),
        vmem((3, rows // 32, 256), BF),
        vmem((8, piece, 256), BF),
        vmem((8, piece, 256), BF),
        vmem((8, piece, 256), BF),
        dma,
        dma,
        *[dma((3,))] * 4,
        *[dma((8,))] * 4,
        *[dma((3,))] * 4,
        dma,
        dma,
    ]


def down(left, right):
    return lax.dot_general(left, right, (((1,), (0,)), ((), ())), preferred_element_type=F32)


def back(left, right):
    return lax.dot_general(left, right, (((1,), (1,)), ((), ())), preferred_element_type=F32)


def outer(left, right):
    return lax.dot_general(left, right, (((0,), (0,)), ((), ())), preferred_element_type=F32)


def flat(value):
    return value.reshape(-1, value.shape[-1])


def beside(rows):
    cells = rows.shape[0]
    column = lax.broadcasted_iota(jnp.int32, (cells, 256), 0) % 64
    left = jnp.where(column == 0, 0.0, pltpu.roll(rows, 1, 0))
    right = jnp.where(column == 63, 0.0, pltpu.roll(rows, cells - 1, 0))
    return left, right


def block_kernel(
    valid,
    gain_from,
    video,
    spatial_weight,
    temporal_weight,
    mix_weight,
    cotangent,
    enc,
    vg,
    gathered_large,
    gathered_small,
    xv,
    sw,
    swt,
    tw,
    mw,
    cv,
    edge_in,
    x3,
    slope,
    active,
    inverse,
    sg_rows,
    sg,
    strided,
    history,
    prior,
    g,
    g_edge,
    g3,
    total,
    gain,
    load_sems,
    edge_s,
    edge_r,
    a2a_s,
    a2a_r,
    next_s,
    next_r,
    prior_s,
    prior_r,
    st_s,
    st_r,
    ge_s,
    ge_r,
    *sum_scratches,
):
    place = Place()
    z, h = place.z, place.h
    above, below = {"height": (h + 15) % 16}, {"height": (h + 1) % 16}
    far = (4, 3, 5, 2, 6, 1, 7)

    loads = [
        pltpu.make_async_copy(cotangent, cv.at[pl.ds(0, 16)], load_sems.at[0]),
        pltpu.make_async_copy(mix_weight, mw, load_sems.at[1]),
        pltpu.make_async_copy(video, xv, load_sems.at[2]),
        pltpu.make_async_copy(spatial_weight, sw, load_sems.at[3]),
        pltpu.make_async_copy(temporal_weight, tw, load_sems.at[4]),
        pltpu.make_async_copy(gain_from, gain, load_sems.at[5]),
    ]
    for load in loads:
        load.start()
    barrier, count = greet(reduce_peers(place) + [above, below])

    cv[pl.ds(16, 2)] = jnp.zeros((2, 64, 256), BF)
    loads[0].wait()
    loads[1].wait()
    for f in (0, 8):
        rows = flat(cv[f : f + 8])
        sum_here = rows.astype(F32)
        for k in range(3):
            sum_here = sum_here + back(flat(cv[f + k : f + k + 8]), mw[k])
        sg_rows[f : f + 8] = sum_here.astype(BF).reshape(8, 64, 256)
    pl.semaphore_wait(barrier, count)

    edges = [
        remote(video.at[:, 7], edge_in.at[0], edge_s.at[0], edge_r.at[0], below),
        remote(video.at[:, 0], edge_in.at[1], edge_s.at[1], edge_r.at[1], above),
    ]
    for copy in edges:
        copy.start()
    a2a = {}
    for d in far:
        peer = (z + d) % 8
        a2a[d] = remote(
            sg_rows.at[pl.ds(2 * peer, 2)], sg.at[pl.ds(0, 2), z], a2a_s.at[d], a2a_r.at[d], place.along_z(d)
        )
        a2a[d].start()
    sg[pl.ds(0, 2), z] = sg_rows[pl.ds(2 * z, 2)]

    start = valid[0]
    loads[2].wait()
    loads[5].wait()
    for f in range(4):
        values = flat(xv[f]).astype(F32)
        values = jnp.where(z * 4 + f >= start, values, 0.0)
        scale = lax.rsqrt(jnp.mean(values * values, axis=-1, keepdims=True) + 1e-06)
        normed = values * scale * gain[...]
        left, right = beside(normed)
        inverse[:, f] = scale.reshape(8, 64, 1)
        x3[1:9, f, :, 0:256] = left.astype(BF).reshape(8, 64, 256)
        x3[1:9, f, :, 256:512] = normed.astype(BF).reshape(8, 64, 256)
        x3[1:9, f, :, 512:768] = right.astype(BF).reshape(8, 64, 256)

    loads[3].wait()

    def forward(row, rows):
        cells = rows * 256
        pre = down(x3[row : row + rows].reshape(cells, 768), sw[0])
        for i in (1, 2):
            pre = pre + down(x3[row + i : row + i + rows].reshape(cells, 768), sw[i])
        q = 1.0 / (1.0 + jnp.exp(-pre))
        active[row : row + rows] = (pre * q).astype(BF).reshape(rows, 4, 64, 256)
        slope[row : row + rows] = (q * (1.0 + pre * (1.0 - q))).reshape(rows, 4, 64, 256)

    forward(1, 2)
    forward(3, 2)
    forward(5, 2)
    frame = z * 4 + lax.broadcasted_iota(jnp.int32, (256, 256), 0) // 64
    for copy in edges:
        copy.wait()
    for side, row, inside in ((0, 0, h > 0), (1, 9, h < 15)):
        values = flat(edge_in[side]).astype(F32)
        values = jnp.where(frame >= start, values, 0.0)
        values = jnp.where(inside, values, 0.0)
        scale = lax.rsqrt(jnp.mean(values * values, axis=-1, keepdims=True) + 1e-06)
        normed = values * scale * gain[...]
        left, right = beside(normed)
        x3[row, :, :, 0:256] = left.astype(BF).reshape(4, 64, 256)
        x3[row, :, :, 256:512] = normed.astype(BF).reshape(4, 64, 256)
        x3[row, :, :, 512:768] = right.astype(BF).reshape(4, 64, 256)
    forward(0, 1)
    forward(7, 1)

    prior_copy = remote(active.at[:, 3], prior, prior_s, prior_r, place.along_z(1))
    prior_copy.start()
    history[pl.ds(0, 2)] = jnp.zeros((2, 64, 256), BF)
    loads[4].wait()
    st = {}

    def send_strided(s):
        for d in far:
            peer = (z + d) % 8
            st[s, d] = remote(
                strided.at[s, peer], history.at[2 + 2 * z + s], st_s.at[s, d], st_r.at[s, d], place.along_z(d)
            )
            st[s, d].start()
        history[2 + 2 * z + s] = strided[s, z]

    sum_here = down(flat(active[:, 3]), tw[0]) + down(flat(active[:, 2]), tw[1]) + down(flat(active[:, 1]), tw[2])
    strided[1] = sum_here.astype(BF).reshape(8, 64, 256)

    for i in range(3):
        for j in range(3):
            swt[i, j * 256 : (j + 1) * 256] = sw[i, j * 256 : (j + 1) * 256].T

    ahead = {0: remote(sg.at[0, z], sg.at[2, z], next_s.at[0], next_r.at[0], place.along_z(7))}
    ahead[0].start()
    for d in (1, 7, 2, 6, 3, 5, 4):
        a2a[d].wait()
        source = (z + 8 - d) % 8
        ahead[d] = remote(sg.at[0, source], sg.at[2, source], next_s.at[d], next_r.at[d], place.along_z(7))
        ahead[d].start()
    send_strided(1)


    def pre_gradient(f, active_gradient):
        value = (active_gradient * flat(slope[:, f])).astype(BF)
        g[:, f] = value.reshape(8, 64, 256)
        left, right = beside(value.astype(F32))
        g3[1:9, f, :, 0:256] = right.astype(BF).reshape(8, 64, 256)
        g3[1:9, f, :, 256:512] = value.reshape(8, 64, 256)
        g3[1:9, f, :, 512:768] = left.astype(BF).reshape(8, 64, 256)

    sg_0, sg_1 = flat(sg[0]), flat(sg[1])
    pre_gradient(0, back(sg_0, tw[1]))
    pre_gradient(1, back(sg_0, tw[0]) + back(sg_1, tw[2]))
    pre_gradient(2, back(sg_1, tw[1]))

    for i in range(3):
        total[i * 768 : (i + 1) * 768] = outer(x3[i : i + 8, 0:3].reshape(1536, 768), g[:, 0:3].reshape(1536, 256))
    base = 9 * 256
    total[base : base + 256] = outer(flat(active[:, 1]), sg_0) + outer(flat(active[:, 3]), sg_1)
    total[base + 256 : base + 512] = outer(flat(active[:, 0]), sg_0) + outer(flat(active[:, 2]), sg_1)

    prior_copy.wait()
    before = jnp.where(z > 0, flat(prior[...]).astype(F32), 0.0).astype(BF)
    sum_here = down(flat(active[:, 1]), tw[0]) + down(flat(active[:, 0]), tw[1]) + down(before, tw[2])
    strided[0] = sum_here.astype(BF).reshape(8, 64, 256)
    send_strided(0)

    for d in range(8):
        ahead[d].wait()
    sg_2 = jnp.where(z < 7, flat(sg[2]).astype(F32), 0.0).astype(BF)
    pre_gradient(3, back(sg_1, tw[0]) + back(sg_2, tw[2]))
    g_edges = started(
        [
            remote(g.at[7], g_edge.at[0], ge_s.at[0], ge_r.at[0], below),
            remote(g.at[0], g_edge.at[1], ge_s.at[1], ge_r.at[1], above),
        ]
    )

    for i in range(3):
        total[i * 768 : (i + 1) * 768] += outer(x3[i : i + 8, 3].reshape(512, 768), flat(g[:, 3]))
    total[base + 512 : base + 768] = outer(flat(active[:, 1]), sg_1) + outer(flat(active[:, 3]), sg_2)
    large = DeviceSum(place, total, 0, gathered_large, sum_scratches[:25])
    small = DeviceSum(place, total, LARGE, gathered_small, sum_scratches[25:])
    large.start_core()

    def clip_gradient(row, gain_sum):
        product = down(g3[row + 2 : row + 4].reshape(512, 768), swt[0])
        for i in (1, 2):
            product = product + down(g3[row + 2 - i : row + 4 - i].reshape(512, 768), swt[i])
        for k in range(2):
            grad = product[k * 256 : (k + 1) * 256]
            values = flat(xv[:, row + k]).astype(F32)
            values = jnp.where(frame >= start, values, 0.0)
            scale = inverse[row + k].reshape(256, 1)
            unit = values * scale
            gain_sum = gain_sum + jnp.sum(grad * unit, axis=0, keepdims=True)
            scaled = grad * gain[...]
            out = scale * (scaled - unit * jnp.mean(scaled * unit, axis=-1, keepdims=True))
            vg[:, row + k] = jnp.where(frame >= start, out, 0.0).astype(BF).reshape(4, 64, 256)
        return gain_sum

    gain_sum = jnp.zeros((1, 256), F32)
    gain_sum = clip_gradient(2, gain_sum)
    gain_sum = clip_gradient(4, gain_sum)
    large.start_first()
    finished(g_edges)
    for side, row, inside in ((0, 0, h > 0), (1, 9, h < 15)):
        values = flat(g_edge[side]).astype(F32)
        values = jnp.where(inside, values, 0.0)
        left, right = beside(values)
        g3[row, :, :, 0:256] = right.astype(BF).reshape(4, 64, 256)
        g3[row, :, :, 256:512] = values.astype(BF).reshape(4, 64, 256)
        g3[row, :, :, 512:768] = left.astype(BF).reshape(4, 64, 256)
    gain_sum = clip_gradient(0, gain_sum)
    gain_sum = clip_gradient(6, gain_sum)
    total[15 * 256 : 16 * 256] = jnp.zeros((256, 256), F32)
    total[15 * 256 : 15 * 256 + 1] = gain_sum

    for s in (1, 0):
        for d in far:
            st[s, d].wait()
    base = 12 * 256
    cot_all = flat(cv[0:16])
    for k in range(3):
        total[base + k * 256 : base + (k + 1) * 256] = outer(flat(history[2 - k : 18 - k]), cot_all)
    small.start_core()
    large.start_second()
    for f in (0, 8):
        sum_here = flat(history[f + 2 : f + 10]).astype(F32)
        for k in range(3):
            sum_here = sum_here + down(flat(history[f + 2 - k : f + 10 - k]), mw[k])
        enc[f : f + 8] = sum_here.astype(BF).reshape(8, 64, 256)
    small.start_first()
    large.start_z()
    small.start_second()
    large.start_z_back()
    small.start_z_at_once()
    large.finish_z_back()
    large.start_second_back()
    small.finish_z_at_once()
    small.start_second_back()
    large.start_first_back()
    small.start_first_back()
    small.start_core_back()
    large.start_core_back()
    small.finish()
    large.finish()


def finish_kernel(scale, enc, vg, large, small, encoded, video_gradient, spatial, temporal, mix, gain_out, ws, wt, wm, wg, sems):
    copies = started(
        [
            pltpu.make_async_copy(vg, video_gradient, sems.at[0]),
            pltpu.make_async_copy(enc, encoded, sems.at[1]),
        ]
    )
    for i in range(9):
        ws[i] = large[i * 256 : (i + 1) * 256].astype(F32) * scale
    copies += started([pltpu.make_async_copy(ws, spatial, sems.at[2])])
    for i in range(3):
        wt[i] = large[(9 + i) * 256 : (10 + i) * 256].astype(F32) * scale
        wm[i] = small[i * 256 : (i + 1) * 256].astype(F32) * scale
    wg[...] = small[3 * 256 : 3 * 256 + 16].astype(F32)[0:1] * scale
    copies += started(
        [
            pltpu.make_async_copy(wt, temporal, sems.at[3]),
            pltpu.make_async_copy(wm, mix, sems.at[4]),
            pltpu.make_async_copy(wg, gain_out, sems.at[5]),
        ]
    )
    finished(copies)


def block_call(valid, gain, video, spatial_weight, temporal_weight, mix_weight, cotangent):
    vmem, dma = pltpu.VMEM, pltpu.SemaphoreType.DMA
    anywhere = pl.BlockSpec(memory_space=pltpu.HBM)
    here = pl.BlockSpec(memory_space=pltpu.VMEM)
    parts = pl.pallas_call(
        block_kernel,
        out_shape=(
            jax.ShapeDtypeStruct((16, 64, 256), BF),
            jax.ShapeDtypeStruct((4, 8, 64, 256), BF),
            jax.ShapeDtypeStruct((LARGE, 256), BF),
            jax.ShapeDtypeStruct((SMALL, 256), BF),
        ),
        in_specs=[pl.BlockSpec(memory_space=pltpu.SMEM)] + [anywhere] * 6,
        out_specs=(here,) * 4,
        scratch_shapes=[
            vmem((4, 8, 64, 256), BF),
            vmem((3, 768, 256), BF),
            vmem((3, 768, 256), BF),
            vmem((3, 256, 256), BF),
            vmem((3, 256, 256), BF),
            vmem((18, 64, 256), BF),
            vmem((2, 4, 64, 256), BF),
            vmem((10, 4, 64, 768), BF),
            vmem((8, 4, 64, 256), F32),
            vmem((8, 4, 64, 256), BF),
            vmem((8, 4, 64, 1), F32),
            vmem((16, 64, 256), BF),
            vmem((3, 8, 64, 256), BF),
            vmem((2, 8, 64, 256), BF),
            vmem((18, 64, 256), BF),
            vmem((8, 64, 256), BF),
            vmem((8, 4, 64, 256), BF),
            vmem((2, 4, 64, 256), BF),
            vmem((10, 4, 64, 768), BF),
            vmem((LARGE + SMALL, 256), F32),
            vmem((1, 256), F32),
            dma((6,)),
            dma((2,)),
            dma((2,)),
            dma((8,)),
            dma((8,)),
            dma((8,)),
            dma((8,)),
            dma,
            dma,
            dma((2, 8)),
            dma((2, 8)),
            dma((2,)),
            dma((2,)),
        ]
        + sum_scratch(LARGE, False)
        + sum_scratch(SMALL, True),
        compiler_params=pltpu.CompilerParams(collective_id=0, has_side_effects=True, vmem_limit_bytes=VMEM_LIMIT),
        name="down_block",
    )(
        valid,
        *[
            pltpu.with_memory_space_constraint(array, pltpu.HBM)
            for array in (gain, video, spatial_weight, temporal_weight, mix_weight, cotangent)
        ],
    )
    scale = 1.0 / math.sqrt(2 * 32 * 128 * 64)
    return pl.pallas_call(
        functools.partial(finish_kernel, scale),
        out_shape=(
            jax.ShapeDtypeStruct((16, 64, 256), BF),
            jax.ShapeDtypeStruct((4, 8, 64, 256), BF),
            jax.ShapeDtypeStruct((9, 256, 256), F32),
            jax.ShapeDtypeStruct((3, 256, 256), F32),
            jax.ShapeDtypeStruct((3, 256, 256), F32),
            jax.ShapeDtypeStruct((1, 256), F32),
        ),
        in_specs=[here] * 4,
        out_specs=(anywhere,) * 6,
        scratch_shapes=[
            vmem((9, 256, 256), F32),
            vmem((3, 256, 256), F32),
            vmem((3, 256, 256), F32),
            vmem((1, 256), F32),
            dma((6,)),
        ],
        compiler_params=pltpu.CompilerParams(vmem_limit_bytes=12 << 20),
        name="write_out",
    )(*parts)


def on_device(video_clip, valid_from, norm_gain, spatial_weight, temporal_weight, mix_weight, cotangent):
    encoded, video_gradient, spatial, temporal, mix, gain = block_call(
        valid_from,
        norm_gain.reshape(1, 256),
        video_clip.reshape(4, 8, 64, 256),
        spatial_weight.reshape(3, 768, 256),
        temporal_weight,
        mix_weight,
        cotangent.reshape(16, 64, 256),
    )
    return (
        encoded.reshape(1, 16, 1, 64, 256),
        video_gradient.reshape(1, 4, 8, 64, 256),
        spatial.reshape(3, 3, 256, 256),
        temporal,
        mix,
        gain.reshape(256),
    )


def solution(mesh):
    return jax.shard_map(
        on_device,
        mesh=mesh,
        in_specs=(
            P("cam", "tm", "height", None, None),
            P("cam"),
            P(),
            P(),
            P(),
            P(),
            P("cam", None, ("height", "tm"), None, None),
        ),
        out_specs=(
            P("cam", None, ("height", "tm"), None, None),
            P("cam", "tm", "height", None, None),
            P(),
            P(),
            P(),
            P(),
        ),
        check_vma=False,
    )
```

```python
import functools
import math

import jax
import jax.numpy as jnp
from jax import lax
from jax.experimental import pallas as pl
from jax.experimental.pallas import tpu as pltpu
from jax.sharding import PartitionSpec as P

MESH = pl.DeviceIdType.MESH
BF = jnp.bfloat16
F32 = jnp.float32
LARGE = 12 * 256
SMALL = 4 * 256
VMEM_LIMIT = 46 << 20


class Place:
    def __init__(self):
        self.z = lax.axis_index("tm")
        self.h = lax.axis_index("height")
        self.c = lax.axis_index("cam")
        self.x = self.h // 4
        self.y = self.h % 4
        self.first = (1 - self.c) * self.x + self.c * self.y
        self.second = (1 - self.c) * self.y + self.c * self.x

    def across(self):
        return {"cam": 1 - self.c}

    def along_first(self, d):
        other = (self.first + d) % 4
        return {"height": (1 - self.c) * (other * 4 + self.y) + self.c * (self.x * 4 + other)}

    def along_second(self, d):
        other = (self.second + d) % 4
        return {"height": (1 - self.c) * (self.x * 4 + other) + self.c * (other * 4 + self.y)}

    def along_x(self, d):
        return {"height": (self.x + d) % 4 * 4 + self.y}

    def along_y(self, d):
        return {"height": self.x * 4 + (self.y + d) % 4}

    def in_plane(self, d):
        return {"height": (self.h + d) % 16}

    def along_z(self, d):
        return {"tm": (self.z + d) % 8}


def remote(src, dst, send, recv, where):
    return pltpu.make_async_remote_copy(
        src_ref=src, dst_ref=dst, send_sem=send, recv_sem=recv, device_id=where, device_id_type=MESH
    )


def greet(peers):
    barrier = pltpu.get_barrier_semaphore()
    for peer in peers:
        pl.semaphore_signal(barrier, inc=1, device_id=peer, device_id_type=MESH)
    return barrier, len(peers)


def reduce_peers(place):
    return [place.across()] + [place.in_plane(d) for d in range(1, 16)] + [place.along_z(d) for d in range(1, 8)]


def block(ref, start, rows):
    return ref.at[pl.ds(pl.multiple_of(start, 16), rows)]


def started(copies):
    for copy in copies:
        copy.start()
    return copies


def finished(copies):
    for copy in copies:
        copy.wait()


ORDER = (2, 1, 3, 0)
UP = (2, 1)
BACK_ORDER = (0, 1, 3, 2)
FAR_FIRST = (4, 3, 5, 2, 6, 1, 7)
PLANE = (10, 5, 15, 7, 13, 9, 11, 6, 14, 8, 2, 12, 4, 3, 1)


def await_bytes(ref, sem):
    pltpu.make_async_copy(ref, ref, sem).wait()


def kind_of(group, e):
    return (2, 3 if e in UP else 1, 1 if e in UP else 3, 0)[group]


class DeviceSum:
    def __init__(self, place, total, base, gathered, scratch):
        self.place, self.total, self.base, self.gathered = place, total, base, gathered
        (
            self.halved,
            self.landed_c,
            self.held_1,
            self.landed_1,
            self.held_2,
            self.landed_2,
            self.own_2,
            self.held_3,
            self.landed_3,
            self.placed_3,
            self.sent,
            self.core_r,
            self.first_r,
            self.second_r,
            self.z_r,
            self.second_back_r,
            self.first_back_r,
            self.core_back_r,
        ) = scratch
        rows = gathered.shape[0]
        self.half, self.n1, self.n2, self.n3 = rows // 2, rows // 8, rows // 32, rows // 256
        self.mine = place.c * self.half

    def rows(self, start):
        return pl.ds(pl.multiple_of(start, 16), self.n2)

    def piece(self, d, e):
        place = self.place
        return self.mine + (place.first + d) % 4 * self.n1 + (place.second + e) % 4 * self.n2

    def send_core(self):
        place = self.place
        other = self.base + (1 - place.c) * self.half
        for group in range(4):
            for i, e in enumerate(ORDER):
                d = kind_of(group, e)
                at = other + (place.second + d) % 4 * self.n1 + (place.first + e) % 4 * self.n2
                self.halved[group * 4 + i] = self.total[self.rows(at), :].astype(BF)
        for group in range(4):
            four = pl.ds(group * 4, 4)
            remote(
                self.halved.at[four], self.landed_c.at[four], self.sent.at[0], self.core_r.at[group], place.across()
            ).start()

    def await_core(self, group):
        await_bytes(self.landed_c.at[pl.ds(group * 4, 4)], self.core_r.at[group])

    def chip_sum(self, group, i, e):
        at = self.base + self.piece(kind_of(group, e), e)
        return self.total[self.rows(at), :] + self.landed_c[group * 4 + i].astype(F32)

    def send_held(self, group, i, value, d):
        k = group * 4 + i
        self.held_1[k] = value.astype(BF)
        remote(
            self.held_1.at[k],
            self.landed_1.at[k],
            self.sent.at[1],
            self.first_r.at[group],
            self.place.along_first(d),
        ).start()

    def send_first(self):
        self.await_core(0)
        for i, e in enumerate(ORDER):
            self.send_held(0, i, self.chip_sum(0, i, e), 1 if e in UP else 3)
        self.await_core(1)
        for i, e in enumerate(ORDER):
            self.send_held(1, i, self.chip_sum(1, i, e), kind_of(1, e))

    def relay_first(self):
        self.await_core(2)
        await_bytes(self.landed_1.at[pl.ds(0, 4)], self.first_r.at[0])
        for i, e in enumerate(ORDER):
            self.send_held(2, i, self.chip_sum(2, i, e) + self.landed_1[i].astype(F32), kind_of(2, e))

    def send_second(self):
        self.await_core(3)
        for group in (1, 2):
            await_bytes(self.landed_1.at[pl.ds(group * 4, 4)], self.first_r.at[group])
        for i, e in enumerate(ORDER):
            sum_here = self.chip_sum(3, i, e)
            sum_here = sum_here + self.landed_1[4 + i].astype(F32) + self.landed_1[8 + i].astype(F32)
            if e == 0:
                self.own_2[...] = sum_here
                continue
            self.held_2[e - 1] = sum_here.astype(BF)
            remote(
                self.held_2.at[e - 1],
                self.landed_2.at[e - 1],
                self.sent.at[2],
                self.second_r,
                self.place.along_second(e),
            ).start()

    def start_z(self):
        await_bytes(self.landed_2, self.second_r)
        sum_here = self.own_2[...]
        for e in (1, 2, 3):
            sum_here = sum_here + self.landed_2[e - 1].astype(F32)
        for k in range(8):
            self.held_3[k, 0 : self.n3] = sum_here[k * self.n3 : (k + 1) * self.n3].astype(BF)
        for d in FAR_FIRST:
            remote(
                self.held_3.at[(self.place.z + d) % 8],
                self.landed_3.at[d - 1],
                self.sent.at[3],
                self.z_r.at[0],
                self.place.along_z(d),
            ).start()

    def start_z_back(self):
        await_bytes(self.landed_3, self.z_r.at[0])
        z = self.place.z
        sum_here = self.held_3[z].astype(F32)
        for d in range(1, 8):
            sum_here = sum_here + self.landed_3[d - 1].astype(F32)
        self.placed_3[z] = sum_here.astype(BF)
        for d in FAR_FIRST:
            remote(
                self.placed_3.at[z], self.placed_3.at[z], self.sent.at[4], self.z_r.at[1], self.place.along_z(d)
            ).start()

    def start_back(self):
        await_bytes(self.landed_3, self.z_r.at[1])
        pieces = [self.placed_3[k].astype(F32)[0 : self.n3] for k in range(8)]
        self.gathered[self.rows(self.piece(0, 0)), :] = jnp.concatenate(pieces).astype(BF)
        for d in (2, 1, 3):
            self.copy_back(self.piece(0, 0), 5, self.second_back_r.at[d // 2 if d == 2 else 0], self.place.along_second(d))
        self.hand_on(0)

    def copy_back(self, start, sent, received, where):
        at = self.gathered.at[self.rows(start)]
        remote(at, at, self.sent.at[sent], received, where).start()

    def hand_on(self, e):
        for d in (1, 3):
            self.copy_back(self.piece(0, 4 - e), 6, self.first_back_r.at[e], self.place.along_first(d))
        self.copy_back(self.piece(0, 4 - e), 7, self.core_back_r, self.place.across())

    def back_second(self, which):
        await_bytes(self.landed_2.at[pl.ds(0, 2 - which)], self.second_back_r.at[which])
        for e in ((1, 3), (2,))[which]:
            self.hand_on(e)

    def back_first(self, e):
        await_bytes(self.landed_1.at[pl.ds(0, 2)], self.first_back_r.at[e])
        for d in (1, 3):
            at = self.piece(4 - d, 4 - e)
            if d == (1 if e in UP else 3):
                self.copy_back(at, 6, self.first_back_r.at[4], self.place.along_first(d))
            self.copy_back(at, 7, self.core_back_r, self.place.across())

    def back_far(self):
        await_bytes(self.landed_1.at[pl.ds(0, 4)], self.first_back_r.at[4])
        for e in BACK_ORDER:
            self.copy_back(self.piece(2, 4 - e), 7, self.core_back_r, self.place.across())

    def finish(self):
        await_bytes(self.landed_c, self.core_back_r)
        for k, ref in enumerate(
            (
                self.halved,
                self.held_1,
                self.held_2,
                self.landed_3,
                self.landed_3,
                self.held_2,
                self.held_1,
                self.halved,
            )
        ):
            await_bytes(ref, self.sent.at[k])


class PlaneSum:
    def __init__(self, place, total, base, gathered, scratch):
        self.place, self.total, self.base, self.gathered = place, total, base, gathered
        self.halved, self.landed_c, self.held, self.landed, self.landed_z, self.sent, self.received = scratch
        rows = gathered.shape[0]
        self.half, self.n = rows // 2, rows // 32
        self.mine = place.c * self.half

    def send_core(self):
        other = pl.multiple_of(self.base + (1 - self.place.c) * self.half, 16)
        self.halved[...] = self.total[pl.ds(other, self.half), :].astype(BF)
        remote(self.halved, self.landed_c, self.sent.at[0], self.received.at[0], self.place.across()).start()

    def send_plane(self):
        await_bytes(self.landed_c, self.received.at[0])
        own = pl.multiple_of(self.base + self.mine, 16)
        value = self.total[pl.ds(own, self.half), :] + self.landed_c[...].astype(F32)
        self.held[...] = value.astype(BF).reshape(16, self.n, 256)
        for d in PLANE:
            remote(
                self.held.at[(self.place.h + d) % 16],
                self.landed.at[d - 1],
                self.sent.at[1],
                self.received.at[1],
                self.place.in_plane(d),
            ).start()

    def start_z(self):
        await_bytes(self.landed, self.received.at[1])
        sum_here = self.held[self.place.h].astype(F32)
        for k in range(15):
            sum_here = sum_here + self.landed[k].astype(F32)
        z = self.place.z
        self.landed_z[z] = sum_here.astype(BF)
        for d in FAR_FIRST:
            remote(
                self.landed_z.at[z], self.landed_z.at[z], self.sent.at[2], self.received.at[2], self.place.along_z(d)
            ).start()

    def start_back(self):
        await_bytes(self.landed_z.at[pl.ds(0, 7)], self.received.at[2])
        sum_here = self.landed_z[0].astype(F32)
        for k in range(1, 8):
            sum_here = sum_here + self.landed_z[k].astype(F32)
        rows = pl.ds(pl.multiple_of(self.mine + self.place.h * self.n, 16), self.n)
        self.gathered[rows, :] = sum_here.astype(BF)
        at = self.gathered.at[rows]
        for d in PLANE:
            remote(at, at, self.sent.at[3], self.received.at[3], self.place.in_plane(d)).start()

    def core_back(self):
        await_bytes(self.landed, self.received.at[3])
        at = self.gathered.at[pl.ds(pl.multiple_of(self.mine, 16), self.half)]
        remote(at, at, self.sent.at[4], self.received.at[4], self.place.across()).start()

    def finish(self):
        await_bytes(self.landed_c, self.received.at[4])
        for k, ref in enumerate((self.halved, self.landed, self.landed_z.at[pl.ds(0, 7)], self.landed, self.halved)):
            await_bytes(ref, self.sent.at[k])


class RowSum:
    def __init__(self, place, scratch):
        self.place = place
        self.slots, self.sent, self.received = scratch[:4], scratch[4], scratch[5]
        self.at = (place.c, place.x, place.y, place.z)
        self.peers = (
            [place.across()],
            [place.along_x(d) for d in (1, 2, 3)],
            [place.along_y(d) for d in (1, 2, 3)],
            [place.along_z(d) for d in range(1, 8)],
        )

    def send(self, stage, value):
        slots, at = self.slots[stage], self.at[stage]
        slots[at] = value
        for peer in self.peers[stage]:
            remote(slots.at[at], slots.at[at], self.sent.at[stage], self.received.at[stage], peer).start()

    def take(self, stage):
        slots = self.slots[stage]
        others = slots.at[pl.ds(0, slots.shape[0] - 1)]
        await_bytes(others, self.received.at[stage])
        await_bytes(others, self.sent.at[stage])
        value = slots[0]
        for k in range(1, slots.shape[0]):
            value = value + slots[k]
        return value

    def step(self, stage):
        self.send(stage + 1, self.take(stage))


def sum_scratch():
    dma, vmem = pltpu.SemaphoreType.DMA, pltpu.VMEM
    n2, n = LARGE // 32, SMALL // 32
    large = [
        vmem((16, n2, 256), BF),
        vmem((16, n2, 256), BF),
        vmem((12, n2, 256), BF),
        vmem((12, n2, 256), BF),
        vmem((3, n2, 256), BF),
        vmem((3, n2, 256), BF),
        vmem((n2, 256), F32),
        vmem((8, 16, 256), BF),
        vmem((7, 16, 256), BF),
        vmem((8, 16, 256), BF),
        dma((8,)),
        dma((4,)),
        dma((3,)),
        dma,
        dma((2,)),
        dma((2,)),
        dma((5,)),
        dma,
    ]
    small = [
        vmem((SMALL // 2, 256), BF),
        vmem((SMALL // 2, 256), BF),
        vmem((16, n, 256), BF),
        vmem((15, n, 256), BF),
        vmem((8, n, 256), BF),
        dma((5,)),
        dma((5,)),
    ]
    row = [vmem((k, 8, 256), F32) for k in (2, 4, 4, 8)] + [dma((4,)), dma((4,))]
    return large, small, row


def down(left, right):
    return lax.dot_general(left, right, (((1,), (0,)), ((), ())), preferred_element_type=F32)


def back(left, right):
    return lax.dot_general(left, right, (((1,), (1,)), ((), ())), preferred_element_type=F32)


def outer(left, right):
    return lax.dot_general(left, right, (((0,), (0,)), ((), ())), preferred_element_type=F32)


def flat(value):
    return value.reshape(-1, value.shape[-1])


def beside(rows):
    cells = rows.shape[0]
    column = lax.broadcasted_iota(jnp.int32, (cells, 256), 0) % 64
    left = jnp.where(column == 0, 0.0, pltpu.roll(rows, 1, 0))
    right = jnp.where(column == 63, 0.0, pltpu.roll(rows, cells - 1, 0))
    return left, right


def block_kernel(
    valid,
    gain_from,
    video,
    spatial_weight,
    temporal_weight,
    mix_weight,
    cotangent,
    enc,
    vg,
    gathered_large,
    gathered_small,
    gain_total,
    xv,
    sw,
    swt,
    tw,
    mw,
    cv,
    edge_in,
    x3,
    slope,
    active,
    inverse,
    sg_rows,
    sg,
    strided,
    history,
    prior,
    g,
    g_edge,
    g3,
    total,
    gain,
    load_sems,
    edge_s,
    edge_r,
    a2a_s,
    a2a_r,
    next_s,
    next_r,
    prior_s,
    prior_r,
    st_s,
    st_r,
    ge_s,
    ge_r,
    hop,
    hop_s,
    hop_r,
    *sum_scratches,
):
    place = Place()
    z, h = place.z, place.h
    above, below = {"height": (h + 15) % 16}, {"height": (h + 1) % 16}
    far = (4, 3, 5, 2, 6, 1, 7)

    loads = [
        pltpu.make_async_copy(cotangent, cv.at[pl.ds(0, 16)], load_sems.at[0]),
        pltpu.make_async_copy(mix_weight, mw, load_sems.at[1]),
        pltpu.make_async_copy(video, xv, load_sems.at[2]),
        pltpu.make_async_copy(spatial_weight, sw, load_sems.at[3]),
        pltpu.make_async_copy(temporal_weight, tw, load_sems.at[4]),
        pltpu.make_async_copy(gain_from, gain, load_sems.at[5]),
    ]
    for load in loads:
        load.start()
    barrier, count = greet(reduce_peers(place) + [above, below])

    cv[pl.ds(16, 2)] = jnp.zeros((2, 64, 256), BF)
    loads[0].wait()
    loads[1].wait()
    for f in (0, 8):
        rows = flat(cv[f : f + 8])
        sum_here = rows.astype(F32)
        for k in range(3):
            sum_here = sum_here + back(flat(cv[f + k : f + k + 8]), mw[k])
        sg_rows[f : f + 8] = sum_here.astype(BF).reshape(8, 64, 256)
    pl.semaphore_wait(barrier, count)

    edges = [
        remote(video.at[:, 7], edge_in.at[0], edge_s.at[0], edge_r.at[0], below),
        remote(video.at[:, 0], edge_in.at[1], edge_s.at[1], edge_r.at[1], above),
    ]
    for copy in edges:
        copy.start()
    half_way = remote(
        sg_rows.at[pl.ds(2 * ((z + 4) % 8), 2)], sg.at[pl.ds(0, 2), z], a2a_s.at[1], a2a_r.at[4], place.along_z(4)
    )
    by_way = [
        remote(sg_rows.at[pl.ds(2 * ((z + 4) % 8), 2)], hop.at[k], hop_s.at[k], hop_r.at[k], place.along_z(d))
        for k, d in ((0, 7), (1, 1))
    ]
    onward = [
        remote(hop.at[k], sg.at[pl.ds(0, 2), (z + d) % 8], hop_s.at[2 + k], a2a_r.at[4], place.along_z(5 if k == 0 else 3))
        for k, d in ((0, 1), (1, 7))
    ]
    low = z // 4 == 0
    relays = ((z + 1) % 8 // 4 == 0, (z + 7) % 8 // 4 == 1)

    @pl.when(place.c == 0)
    def _():
        half_way.start()

    @pl.when(jnp.logical_and(place.c == 1, low))
    def _():
        by_way[0].start()

    @pl.when(jnp.logical_and(place.c == 1, jnp.logical_not(low)))
    def _():
        by_way[1].start()

    a2a = {}
    for d in (3, 5, 2, 6, 1, 7):
        peer = (z + d) % 8
        a2a[d] = remote(
            sg_rows.at[pl.ds(2 * peer, 2)], sg.at[pl.ds(0, 2), z], a2a_s.at[0], a2a_r.at[d], place.along_z(d)
        )
        a2a[d].start()
    sg[pl.ds(0, 2), z] = sg_rows[pl.ds(2 * z, 2)]

    loads[2].wait()
    loads[5].wait()
    start = valid[0]
    for f in range(4):
        values = flat(xv[f]).astype(F32)
        values = jnp.where(z * 4 + f >= start, values, 0.0)
        scale = lax.rsqrt(jnp.mean(values * values, axis=-1, keepdims=True) + 1e-06)
        normed = values * scale * gain[...]
        left, right = beside(normed)
        inverse[:, f] = scale.reshape(8, 64, 1)
        x3[1:9, f, :, 0:256] = left.astype(BF).reshape(8, 64, 256)
        x3[1:9, f, :, 256:512] = normed.astype(BF).reshape(8, 64, 256)
        x3[1:9, f, :, 512:768] = right.astype(BF).reshape(8, 64, 256)

    loads[3].wait()

    def forward(row, rows):
        cells = rows * 256
        pre = down(x3[row : row + rows].reshape(cells, 768), sw[0])
        for i in (1, 2):
            pre = pre + down(x3[row + i : row + i + rows].reshape(cells, 768), sw[i])
        q = 1.0 / (1.0 + jnp.exp(-pre))
        active[row : row + rows] = (pre * q).astype(BF).reshape(rows, 4, 64, 256)
        slope[row : row + rows] = (q * (1.0 + pre * (1.0 - q))).reshape(rows, 4, 64, 256)

    forward(1, 2)
    forward(3, 2)
    forward(5, 2)
    frame = z * 4 + lax.broadcasted_iota(jnp.int32, (256, 256), 0) // 64
    for k in (0, 1):

        @pl.when(jnp.logical_and(place.c == 1, relays[k]))
        def _():
            by_way[k].wait_recv()
            onward[k].start()

    for copy in edges:
        copy.wait()
    for side, row, inside in ((0, 0, h > 0), (1, 9, h < 15)):
        values = flat(edge_in[side]).astype(F32)
        values = jnp.where(frame >= start, values, 0.0)
        values = jnp.where(inside, values, 0.0)
        scale = lax.rsqrt(jnp.mean(values * values, axis=-1, keepdims=True) + 1e-06)
        normed = values * scale * gain[...]
        left, right = beside(normed)
        x3[row, :, :, 0:256] = left.astype(BF).reshape(4, 64, 256)
        x3[row, :, :, 256:512] = normed.astype(BF).reshape(4, 64, 256)
        x3[row, :, :, 512:768] = right.astype(BF).reshape(4, 64, 256)
    forward(0, 1)
    forward(7, 1)

    prior_copy = remote(active.at[:, 3], prior, prior_s, prior_r, place.along_z(1))

    @pl.when(z < 7)
    def _():
        prior_copy.start()


    history[pl.ds(0, 2)] = jnp.zeros((2, 64, 256), BF)
    loads[4].wait()
    st = {}

    def send_strided(s):
        for d in far:
            peer = (z + d) % 8
            st[s, d] = remote(
                strided.at[s, peer], history.at[2 + 2 * z + s], st_s, st_r, place.along_z(d)
            )
            st[s, d].start()
        history[2 + 2 * z + s] = strided[s, z]

    sum_here = down(flat(active[:, 3]), tw[0]) + down(flat(active[:, 2]), tw[1]) + down(flat(active[:, 1]), tw[2])
    strided[1] = sum_here.astype(BF).reshape(8, 64, 256)

    for i in range(3):
        for j in range(3):
            swt[i, j * 256 : (j + 1) * 256] = sw[i, j * 256 : (j + 1) * 256].T

    ahead = {}

    def send_ahead(d):
        source = (z + 8 - d) % 8
        ahead[d] = remote(sg.at[0, source], sg.at[2, source], next_s, next_r, place.along_z(7))

        @pl.when(z > 0)
        def _():
            ahead[d].start()

    send_ahead(0)
    for d in (1, 7, 2, 6, 3, 5):
        a2a[d].wait_recv()
        send_ahead(d)
    half_way.wait_recv()
    send_ahead(4)


    def pre_gradient(f, active_gradient):
        value = (active_gradient * flat(slope[:, f])).astype(BF)
        g[:, f] = value.reshape(8, 64, 256)
        left, right = beside(value.astype(F32))
        g3[1:9, f, :, 0:256] = right.astype(BF).reshape(8, 64, 256)
        g3[1:9, f, :, 256:512] = value.reshape(8, 64, 256)
        g3[1:9, f, :, 512:768] = left.astype(BF).reshape(8, 64, 256)

    sg_0, sg_1 = flat(sg[0]), flat(sg[1])
    pre_gradient(0, back(sg_0, tw[1]))
    pre_gradient(1, back(sg_0, tw[0]) + back(sg_1, tw[2]))
    pre_gradient(2, back(sg_1, tw[1]))

    for i in range(3):
        total[i * 768 : (i + 1) * 768] = outer(x3[i : i + 8, 0:3].reshape(1536, 768), g[:, 0:3].reshape(1536, 256))
    base = 9 * 256
    total[base : base + 256] = outer(flat(active[:, 1]), sg_0) + outer(flat(active[:, 3]), sg_1)
    total[base + 256 : base + 512] = outer(flat(active[:, 0]), sg_0) + outer(flat(active[:, 2]), sg_1)

    @pl.when(place.c == 0)
    def _():
        half_way.wait_send()

    @pl.when(jnp.logical_and(place.c == 1, low))
    def _():
        by_way[0].wait_send()

    @pl.when(jnp.logical_and(place.c == 1, jnp.logical_not(low)))
    def _():
        by_way[1].wait_send()

    for k in (0, 1):

        @pl.when(jnp.logical_and(place.c == 1, relays[k]))
        def _():
            onward[k].wait_send()

    @pl.when(z > 0)
    def _():
        await_bytes(sg.at[2], next_s)

    @pl.when(z < 7)
    def _():
        await_bytes(sg.at[2], next_r)

    send_strided(1)
    sg_2 = jnp.where(z < 7, flat(sg[2]).astype(F32), 0.0).astype(BF)
    pre_gradient(3, back(sg_1, tw[0]) + back(sg_2, tw[2]))
    for i in range(3):
        total[i * 768 : (i + 1) * 768] += outer(x3[i : i + 8, 3].reshape(512, 768), flat(g[:, 3]))
    total[base + 512 : base + 768] = outer(flat(active[:, 1]), sg_1) + outer(flat(active[:, 3]), sg_2)
    large = DeviceSum(place, total, 0, gathered_large, sum_scratches[:18])
    small = PlaneSum(place, total, LARGE, gathered_small, sum_scratches[18:25])
    row_sum = RowSum(place, sum_scratches[25:])
    large.send_core()
    def clip_gradient(row, gain_sum):
        product = down(g3[row + 2 : row + 4].reshape(512, 768), swt[0])
        for i in (1, 2):
            product = product + down(g3[row + 2 - i : row + 4 - i].reshape(512, 768), swt[i])
        for k in range(2):
            grad = product[k * 256 : (k + 1) * 256]
            values = flat(xv[:, row + k]).astype(F32)
            values = jnp.where(frame >= start, values, 0.0)
            scale = inverse[row + k].reshape(256, 1)
            unit = values * scale
            gain_sum = gain_sum + jnp.sum(grad * unit, axis=0, keepdims=True)
            scaled = grad * gain[...]
            out = scale * (scaled - unit * jnp.mean(scaled * unit, axis=-1, keepdims=True))
            vg[:, row + k] = jnp.where(frame >= start, out, 0.0).astype(BF).reshape(4, 64, 256)
        return gain_sum

    gain_sum = jnp.zeros((1, 256), F32)
    large.send_first()
    @pl.when(z < 7)
    def _():
        prior_copy.wait_send()

    @pl.when(z > 0)
    def _():
        prior_copy.wait_recv()

    before = jnp.where(z > 0, flat(prior[...]).astype(F32), 0.0).astype(BF)
    sum_here = down(flat(active[:, 1]), tw[0]) + down(flat(active[:, 0]), tw[1]) + down(before, tw[2])
    strided[0] = sum_here.astype(BF).reshape(8, 64, 256)
    send_strided(0)
    gain_sum = clip_gradient(2, gain_sum)
    large.relay_first()
    gain_sum = clip_gradient(4, gain_sum)
    large.send_second()
    g_edges = started(
        [
            remote(g.at[7], g_edge.at[0], ge_s.at[0], ge_r.at[0], below),
            remote(g.at[0], g_edge.at[1], ge_s.at[1], ge_r.at[1], above),
        ]
    )
    large.start_z()
    finished(g_edges)
    for side, row, inside in ((0, 0, h > 0), (1, 9, h < 15)):
        values = flat(g_edge[side]).astype(F32)
        values = jnp.where(inside, values, 0.0)
        left, right = beside(values)
        g3[row, :, :, 0:256] = right.astype(BF).reshape(4, 64, 256)
        g3[row, :, :, 256:512] = values.astype(BF).reshape(4, 64, 256)
        g3[row, :, :, 512:768] = left.astype(BF).reshape(4, 64, 256)
    gain_sum = clip_gradient(0, gain_sum)
    await_bytes(history.at[pl.ds(0, 14)], st_r)
    base = 12 * 256
    cot_all = flat(cv[0:16])
    for k in range(3):
        total[base + k * 256 : base + (k + 1) * 256] = outer(flat(history[2 - k : 18 - k]), cot_all)
    total[15 * 256 : 16 * 256] = jnp.zeros((256, 256), F32)
    small.send_core()
    gain_sum = clip_gradient(6, gain_sum)
    row_sum.send(0, jnp.broadcast_to(gain_sum, (8, 256)))
    small.send_plane()
    large.start_z_back()
    for f in (0, 8):
        sum_here = flat(history[f + 2 : f + 10]).astype(F32)
        for k in range(3):
            sum_here = sum_here + down(flat(history[f + 2 - k : f + 10 - k]), mw[k])
        enc[f : f + 8] = sum_here.astype(BF).reshape(8, 64, 256)
    row_sum.step(0)
    large.start_back()
    row_sum.step(1)
    small.start_z()
    large.back_second(0)
    large.back_first(0)
    large.back_second(1)
    row_sum.step(2)
    large.back_first(1)
    large.back_first(3)
    large.back_first(2)
    small.start_back()
    large.back_far()
    gain_total[...] = row_sum.take(3)
    small.core_back()
    await_bytes(sg_rows.at[pl.ds(0, 12)], a2a_s.at[0])
    await_bytes(strided.at[:, pl.ds(0, 7)], st_s)
    large.finish()
    small.finish()


def finish_kernel(scale, enc, vg, large, small, gain_total, encoded, video_gradient, spatial, temporal, mix, gain_out, ws, wt, wm, wg, sems):
    copies = started(
        [
            pltpu.make_async_copy(vg, video_gradient, sems.at[0]),
            pltpu.make_async_copy(enc, encoded, sems.at[1]),
        ]
    )
    for i in range(9):
        ws[i] = large[i * 256 : (i + 1) * 256].astype(F32) * scale
    copies += started([pltpu.make_async_copy(ws, spatial, sems.at[2])])
    for i in range(3):
        wt[i] = large[(9 + i) * 256 : (10 + i) * 256].astype(F32) * scale
        wm[i] = small[i * 256 : (i + 1) * 256].astype(F32) * scale
    wg[...] = gain_total[0:1] * scale
    copies += started(
        [
            pltpu.make_async_copy(wt, temporal, sems.at[3]),
            pltpu.make_async_copy(wm, mix, sems.at[4]),
            pltpu.make_async_copy(wg, gain_out, sems.at[5]),
        ]
    )
    finished(copies)


def block_call(valid, gain, video, spatial_weight, temporal_weight, mix_weight, cotangent):
    vmem, dma = pltpu.VMEM, pltpu.SemaphoreType.DMA
    anywhere = pl.BlockSpec(memory_space=pltpu.HBM)
    here = pl.BlockSpec(memory_space=pltpu.VMEM)
    parts = pl.pallas_call(
        block_kernel,
        out_shape=(
            jax.ShapeDtypeStruct((16, 64, 256), BF),
            jax.ShapeDtypeStruct((4, 8, 64, 256), BF),
            jax.ShapeDtypeStruct((LARGE, 256), BF),
            jax.ShapeDtypeStruct((SMALL, 256), BF),
            jax.ShapeDtypeStruct((8, 256), F32),
        ),
        in_specs=[pl.BlockSpec(memory_space=pltpu.SMEM)] + [anywhere] * 6,
        out_specs=(here,) * 5,
        scratch_shapes=[
            vmem((4, 8, 64, 256), BF),
            vmem((3, 768, 256), BF),
            vmem((3, 768, 256), BF),
            vmem((3, 256, 256), BF),
            vmem((3, 256, 256), BF),
            vmem((18, 64, 256), BF),
            vmem((2, 4, 64, 256), BF),
            vmem((10, 4, 64, 768), BF),
            vmem((8, 4, 64, 256), F32),
            vmem((8, 4, 64, 256), BF),
            vmem((8, 4, 64, 1), F32),
            vmem((16, 64, 256), BF),
            vmem((3, 8, 64, 256), BF),
            vmem((2, 8, 64, 256), BF),
            vmem((18, 64, 256), BF),
            vmem((8, 64, 256), BF),
            vmem((8, 4, 64, 256), BF),
            vmem((2, 4, 64, 256), BF),
            vmem((10, 4, 64, 768), BF),
            vmem((LARGE + SMALL, 256), F32),
            vmem((1, 256), F32),
            dma((6,)),
            dma((2,)),
            dma((2,)),
            dma((2,)),
            dma((8,)),
            dma,
            dma,
            dma,
            dma,
            dma,
            dma,
            dma((2,)),
            dma((2,)),
            vmem((2, 2, 64, 256), BF),
            dma((4,)),
            dma((2,)),
        ]
        + sum(sum_scratch(), []),
        compiler_params=pltpu.CompilerParams(collective_id=0, has_side_effects=True, vmem_limit_bytes=VMEM_LIMIT),
        name="down_block",
    )(
        valid,
        *[
            pltpu.with_memory_space_constraint(array, pltpu.HBM)
            for array in (gain, video, spatial_weight, temporal_weight, mix_weight, cotangent)
        ],
    )
    scale = 1.0 / math.sqrt(2 * 32 * 128 * 64)
    return pl.pallas_call(
        functools.partial(finish_kernel, scale),
        out_shape=(
            jax.ShapeDtypeStruct((16, 64, 256), BF),
            jax.ShapeDtypeStruct((4, 8, 64, 256), BF),
            jax.ShapeDtypeStruct((9, 256, 256), F32),
            jax.ShapeDtypeStruct((3, 256, 256), F32),
            jax.ShapeDtypeStruct((3, 256, 256), F32),
            jax.ShapeDtypeStruct((1, 256), F32),
        ),
        in_specs=[here] * 5,
        out_specs=(anywhere,) * 6,
        scratch_shapes=[
            vmem((9, 256, 256), F32),
            vmem((3, 256, 256), F32),
            vmem((3, 256, 256), F32),
            vmem((1, 256), F32),
            dma((6,)),
        ],
        compiler_params=pltpu.CompilerParams(vmem_limit_bytes=12 << 20),
        name="write_out",
    )(*parts)


def on_device(video_clip, valid_from, norm_gain, spatial_weight, temporal_weight, mix_weight, cotangent):
    encoded, video_gradient, spatial, temporal, mix, gain = block_call(
        valid_from,
        norm_gain.reshape(1, 256),
        video_clip.reshape(4, 8, 64, 256),
        spatial_weight.reshape(3, 768, 256),
        temporal_weight,
        mix_weight,
        cotangent.reshape(16, 64, 256),
    )
    return (
        encoded.reshape(1, 16, 1, 64, 256),
        video_gradient.reshape(1, 4, 8, 64, 256),
        spatial.reshape(3, 3, 256, 256),
        temporal,
        mix,
        gain.reshape(256),
    )


def solution(mesh):
    return jax.shard_map(
        on_device,
        mesh=mesh,
        in_specs=(
            P("cam", "tm", "height", None, None),
            P("cam"),
            P(),
            P(),
            P(),
            P(),
            P("cam", None, ("height", "tm"), None, None),
        ),
        out_specs=(
            P("cam", None, ("height", "tm"), None, None),
            P("cam", "tm", "height", None, None),
            P(),
            P(),
            P(),
            P(),
        ),
        check_vma=False,
    )
```

```python
import functools
import math

import jax
import jax.numpy as jnp
from jax import lax
from jax.experimental import pallas as pl
from jax.experimental.pallas import tpu as pltpu
from jax.sharding import PartitionSpec as P

MESH = pl.DeviceIdType.MESH
BF = jnp.bfloat16
F32 = jnp.float32
LARGE = 12 * 256
SMALL = 3 * 256
VMEM_LIMIT = 46 << 20


class Place:
    def __init__(self):
        self.z = lax.axis_index("tm")
        self.h = lax.axis_index("height")
        self.c = lax.axis_index("cam")
        self.x = self.h // 4
        self.y = self.h % 4
        self.first = (1 - self.c) * self.x + self.c * self.y
        self.second = (1 - self.c) * self.y + self.c * self.x

    def across(self):
        return {"cam": 1 - self.c}

    def along_first(self, d):
        other = (self.first + d) % 4
        return {"height": (1 - self.c) * (other * 4 + self.y) + self.c * (self.x * 4 + other)}

    def along_second(self, d):
        other = (self.second + d) % 4
        return {"height": (1 - self.c) * (self.x * 4 + other) + self.c * (other * 4 + self.y)}

    def along_x(self, d):
        return {"height": (self.x + d) % 4 * 4 + self.y}

    def along_y(self, d):
        return {"height": self.x * 4 + (self.y + d) % 4}

    def in_plane(self, d):
        return {"height": (self.h + d) % 16}

    def along_z(self, d):
        return {"tm": (self.z + d) % 8}


def remote(src, dst, send, recv, where):
    return pltpu.make_async_remote_copy(
        src_ref=src, dst_ref=dst, send_sem=send, recv_sem=recv, device_id=where, device_id_type=MESH
    )


def greet(peers):
    barrier = pltpu.get_barrier_semaphore()
    for peer in peers:
        pl.semaphore_signal(barrier, inc=1, device_id=peer, device_id_type=MESH)
    return barrier, len(peers)


def reduce_peers(place):
    return [place.across()] + [place.in_plane(d) for d in range(1, 16)] + [place.along_z(d) for d in range(1, 8)]


def block(ref, start, rows):
    return ref.at[pl.ds(pl.multiple_of(start, 16), rows)]


def started(copies):
    for copy in copies:
        copy.start()
    return copies


def finished(copies):
    for copy in copies:
        copy.wait()


ORDER = (2, 1, 3, 0)
UP = (2, 1)
BACK_ORDER = (0, 1, 3, 2)
FAR_FIRST = (4, 3, 5, 2, 6, 1, 7)
PLANE = (10, 5, 15, 7, 13, 9, 11, 6, 14, 8, 2, 12, 4, 3, 1)


def await_bytes(ref, sem):
    pltpu.make_async_copy(ref, ref, sem).wait()


def kind_of(group, e):
    return (2, 3 if e in UP else 1, 1 if e in UP else 3, 0)[group]


class DeviceSum:
    def __init__(self, place, total, base, gathered, scratch):
        self.place, self.total, self.base, self.gathered = place, total, base, gathered
        (
            self.halved,
            self.landed_c,
            self.held_1,
            self.landed_1,
            self.held_2,
            self.landed_2,
            self.own_2,
            self.held_3,
            self.landed_3,
            self.placed_3,
            self.sent,
            self.core_r,
            self.first_r,
            self.second_r,
            self.z_r,
            self.second_back_r,
            self.first_back_r,
            self.core_back_r,
        ) = scratch
        rows = gathered.shape[0]
        self.half, self.n1, self.n2, self.n3 = rows // 2, rows // 8, rows // 32, rows // 256
        self.mine = place.c * self.half

    def rows(self, start):
        return pl.ds(pl.multiple_of(start, 16), self.n2)

    def piece(self, d, e):
        place = self.place
        return self.mine + (place.first + d) % 4 * self.n1 + (place.second + e) % 4 * self.n2

    def send_core(self):
        place = self.place
        other = self.base + (1 - place.c) * self.half
        for group in range(4):
            for i, e in enumerate(ORDER):
                d = kind_of(group, e)
                at = other + (place.second + d) % 4 * self.n1 + (place.first + e) % 4 * self.n2
                self.halved[group * 4 + i] = self.total[self.rows(at), :].astype(BF)
        for group in range(4):
            four = pl.ds(group * 4, 4)
            remote(
                self.halved.at[four], self.landed_c.at[four], self.sent.at[0], self.core_r.at[group], place.across()
            ).start()

    def await_core(self, group):
        await_bytes(self.landed_c.at[pl.ds(group * 4, 4)], self.core_r.at[group])

    def chip_sum(self, group, i, e):
        at = self.base + self.piece(kind_of(group, e), e)
        return self.total[self.rows(at), :] + self.landed_c[group * 4 + i].astype(F32)

    def send_held(self, group, i, value, d):
        k = group * 4 + i
        self.held_1[k] = value.astype(BF)
        remote(
            self.held_1.at[k],
            self.landed_1.at[k],
            self.sent.at[1],
            self.first_r.at[group],
            self.place.along_first(d),
        ).start()

    def send_first(self):
        self.await_core(0)
        for i, e in enumerate(ORDER):
            self.send_held(0, i, self.chip_sum(0, i, e), 1 if e in UP else 3)
        self.await_core(1)
        for i, e in enumerate(ORDER):
            self.send_held(1, i, self.chip_sum(1, i, e), kind_of(1, e))

    def relay_first(self):
        self.await_core(2)
        await_bytes(self.landed_1.at[pl.ds(0, 4)], self.first_r.at[0])
        for i, e in enumerate(ORDER):
            self.send_held(2, i, self.chip_sum(2, i, e) + self.landed_1[i].astype(F32), kind_of(2, e))

    def send_second(self):
        self.await_core(3)
        for group in (1, 2):
            await_bytes(self.landed_1.at[pl.ds(group * 4, 4)], self.first_r.at[group])
        for i, e in enumerate(ORDER):
            sum_here = self.chip_sum(3, i, e)
            sum_here = sum_here + self.landed_1[4 + i].astype(F32) + self.landed_1[8 + i].astype(F32)
            if e == 0:
                self.own_2[...] = sum_here
                continue
            self.held_2[e - 1] = sum_here.astype(BF)
            remote(
                self.held_2.at[e - 1],
                self.landed_2.at[e - 1],
                self.sent.at[2],
                self.second_r,
                self.place.along_second(e),
            ).start()

    def start_z(self):
        await_bytes(self.landed_2, self.second_r)
        sum_here = self.own_2[...]
        for e in (1, 2, 3):
            sum_here = sum_here + self.landed_2[e - 1].astype(F32)
        for k in range(8):
            self.held_3[k, 0 : self.n3] = sum_here[k * self.n3 : (k + 1) * self.n3].astype(BF)
        for d in FAR_FIRST:
            remote(
                self.held_3.at[(self.place.z + d) % 8],
                self.landed_3.at[d - 1],
                self.sent.at[3],
                self.z_r.at[0],
                self.place.along_z(d),
            ).start()

    def start_z_back(self):
        await_bytes(self.landed_3, self.z_r.at[0])
        z = self.place.z
        sum_here = self.held_3[z].astype(F32)
        for d in range(1, 8):
            sum_here = sum_here + self.landed_3[d - 1].astype(F32)
        self.placed_3[z] = sum_here.astype(BF)
        for d in FAR_FIRST:
            remote(
                self.placed_3.at[z], self.placed_3.at[z], self.sent.at[4], self.z_r.at[1], self.place.along_z(d)
            ).start()

    def start_back(self):
        await_bytes(self.landed_3, self.z_r.at[1])
        pieces = [self.placed_3[k].astype(F32)[0 : self.n3] for k in range(8)]
        self.gathered[self.rows(self.piece(0, 0)), :] = jnp.concatenate(pieces).astype(BF)
        for d in (2, 1, 3):
            self.copy_back(self.piece(0, 0), 5, self.second_back_r.at[d // 2 if d == 2 else 0], self.place.along_second(d))
        self.hand_on(0)

    def copy_back(self, start, sent, received, where):
        at = self.gathered.at[self.rows(start)]
        remote(at, at, self.sent.at[sent], received, where).start()

    def hand_on(self, e):
        for d in (1, 3):
            self.copy_back(self.piece(0, 4 - e), 6, self.first_back_r.at[e], self.place.along_first(d))
        self.copy_back(self.piece(0, 4 - e), 7, self.core_back_r, self.place.across())

    def back_second(self, which):
        await_bytes(self.landed_2.at[pl.ds(0, 2 - which)], self.second_back_r.at[which])
        for e in ((1, 3), (2,))[which]:
            self.hand_on(e)

    def back_first(self, e):
        await_bytes(self.landed_1.at[pl.ds(0, 2)], self.first_back_r.at[e])
        for d in (1, 3):
            at = self.piece(4 - d, 4 - e)
            if d == (1 if e in UP else 3):
                self.copy_back(at, 6, self.first_back_r.at[4], self.place.along_first(d))
            self.copy_back(at, 7, self.core_back_r, self.place.across())

    def back_far(self):
        await_bytes(self.landed_1.at[pl.ds(0, 4)], self.first_back_r.at[4])
        for e in BACK_ORDER:
            self.copy_back(self.piece(2, 4 - e), 7, self.core_back_r, self.place.across())

    def finish(self):
        await_bytes(self.landed_c, self.core_back_r)
        for k, ref in enumerate(
            (
                self.halved,
                self.held_1,
                self.held_2,
                self.landed_3,
                self.landed_3,
                self.held_2,
                self.held_1,
                self.halved,
            )
        ):
            await_bytes(ref, self.sent.at[k])


class PlaneSum:
    def __init__(self, place, total, base, gathered, scratch):
        self.place, self.total, self.base, self.gathered = place, total, base, gathered
        self.halved, self.landed_c, self.held, self.landed, self.landed_z, self.sent, self.received = scratch
        self.n = gathered.shape[1]
        self.half = 16 * self.n
        self.mine = place.c * self.half

    def send_core(self):
        other = pl.multiple_of(self.base + (1 - self.place.c) * self.half, 16)
        self.halved[...] = self.total[pl.ds(other, self.half), :].reshape(16, self.n, 256).astype(BF)
        remote(self.halved, self.landed_c, self.sent.at[0], self.received.at[0], self.place.across()).start()

    def send_plane(self):
        await_bytes(self.landed_c, self.received.at[0])
        own = pl.multiple_of(self.base + self.mine, 16)
        value = self.total[pl.ds(own, self.half), :].reshape(16, self.n, 256) + self.landed_c[...].astype(F32)
        self.held[...] = value.astype(BF)
        for d in PLANE:
            remote(
                self.held.at[(self.place.h + d) % 16],
                self.landed.at[d - 1],
                self.sent.at[1],
                self.received.at[1],
                self.place.in_plane(d),
            ).start()

    def start_z(self):
        await_bytes(self.landed, self.received.at[1])
        sum_here = self.held[self.place.h].astype(F32)
        for k in range(15):
            sum_here = sum_here + self.landed[k].astype(F32)
        z = self.place.z
        self.landed_z[z] = sum_here.astype(BF)
        for d in FAR_FIRST:
            remote(
                self.landed_z.at[z], self.landed_z.at[z], self.sent.at[2], self.received.at[2], self.place.along_z(d)
            ).start()

    def start_back(self):
        await_bytes(self.landed_z.at[pl.ds(0, 7)], self.received.at[2])
        sum_here = self.landed_z[0].astype(F32)
        for k in range(1, 8):
            sum_here = sum_here + self.landed_z[k].astype(F32)
        mine = self.place.c * 16 + self.place.h
        self.gathered[mine] = sum_here.astype(BF)
        at = self.gathered.at[mine]
        for d in PLANE:
            remote(at, at, self.sent.at[3], self.received.at[3], self.place.in_plane(d)).start()

    def core_back(self):
        await_bytes(self.landed, self.received.at[3])
        at = self.gathered.at[pl.ds(self.place.c * 16, 16)]
        remote(at, at, self.sent.at[4], self.received.at[4], self.place.across()).start()

    def finish(self):
        await_bytes(self.landed_c, self.received.at[4])
        for k, ref in enumerate((self.halved, self.landed, self.landed_z.at[pl.ds(0, 7)], self.landed, self.halved)):
            await_bytes(ref, self.sent.at[k])


class RowSum:
    def __init__(self, place, scratch):
        self.place = place
        self.slots, self.sent, self.received = scratch[:4], scratch[4], scratch[5]
        self.at = (place.c, place.x, place.y, place.z)
        self.peers = (
            [place.across()],
            [place.along_x(d) for d in (1, 2, 3)],
            [place.along_y(d) for d in (1, 2, 3)],
            [place.along_z(d) for d in range(1, 8)],
        )

    def send(self, stage, value):
        slots, at = self.slots[stage], self.at[stage]
        slots[at] = value
        for peer in self.peers[stage]:
            remote(slots.at[at], slots.at[at], self.sent.at[stage], self.received.at[stage], peer).start()

    def take(self, stage):
        slots = self.slots[stage]
        others = slots.at[pl.ds(0, slots.shape[0] - 1)]
        await_bytes(others, self.received.at[stage])
        await_bytes(others, self.sent.at[stage])
        value = slots[0]
        for k in range(1, slots.shape[0]):
            value = value + slots[k]
        return value

    def step(self, stage):
        self.send(stage + 1, self.take(stage))


def sum_scratch():
    dma, vmem = pltpu.SemaphoreType.DMA, pltpu.VMEM
    n2, n = LARGE // 32, SMALL // 32
    large = [
        vmem((16, n2, 256), BF),
        vmem((16, n2, 256), BF),
        vmem((12, n2, 256), BF),
        vmem((12, n2, 256), BF),
        vmem((3, n2, 256), BF),
        vmem((3, n2, 256), BF),
        vmem((n2, 256), F32),
        vmem((8, 16, 256), BF),
        vmem((7, 16, 256), BF),
        vmem((8, 16, 256), BF),
        dma((8,)),
        dma((4,)),
        dma((3,)),
        dma,
        dma((2,)),
        dma((2,)),
        dma((5,)),
        dma,
    ]
    small = [
        vmem((16, n, 256), BF),
        vmem((16, n, 256), BF),
        vmem((16, n, 256), BF),
        vmem((15, n, 256), BF),
        vmem((8, n, 256), BF),
        dma((5,)),
        dma((5,)),
    ]
    row = [vmem((k, 8, 256), F32) for k in (2, 4, 4, 8)] + [dma((4,)), dma((4,))]
    return large, small, row


def down(left, right):
    return lax.dot_general(left, right, (((1,), (0,)), ((), ())), preferred_element_type=F32)


def back(left, right):
    return lax.dot_general(left, right, (((1,), (1,)), ((), ())), preferred_element_type=F32)


def outer(left, right):
    return lax.dot_general(left, right, (((0,), (0,)), ((), ())), preferred_element_type=F32)


def flat(value):
    return value.reshape(-1, value.shape[-1])


def beside(rows):
    cells = rows.shape[0]
    column = lax.broadcasted_iota(jnp.int32, (cells, 256), 0) % 64
    left = jnp.where(column == 0, 0.0, pltpu.roll(rows, 1, 0))
    right = jnp.where(column == 63, 0.0, pltpu.roll(rows, cells - 1, 0))
    return left, right


def block_kernel(
    valid,
    gain_from,
    video,
    spatial_weight,
    temporal_weight,
    mix_weight,
    cotangent,
    enc,
    vg,
    gathered_large,
    gathered_small,
    gain_total,
    xv,
    sw,
    swt,
    tw,
    mw,
    cv,
    edge_in,
    x3,
    slope,
    active,
    inverse,
    sg_rows,
    sg,
    strided,
    history,
    prior,
    g,
    g_edge,
    g3,
    total,
    gain,
    load_sems,
    edge_s,
    edge_r,
    a2a_s,
    a2a_r,
    next_s,
    next_r,
    prior_s,
    prior_r,
    st_s,
    st_r,
    ge_s,
    ge_r,
    hop,
    hop_s,
    hop_r,
    *sum_scratches,
):
    place = Place()
    z, h = place.z, place.h
    above, below = {"height": (h + 15) % 16}, {"height": (h + 1) % 16}
    far = (4, 3, 5, 2, 6, 1, 7)

    loads = [
        pltpu.make_async_copy(cotangent, cv.at[pl.ds(0, 16)], load_sems.at[0]),
        pltpu.make_async_copy(mix_weight, mw, load_sems.at[1]),
        pltpu.make_async_copy(video, xv, load_sems.at[2]),
        pltpu.make_async_copy(spatial_weight, sw, load_sems.at[3]),
        pltpu.make_async_copy(temporal_weight, tw, load_sems.at[4]),
        pltpu.make_async_copy(gain_from, gain, load_sems.at[5]),
    ]
    for load in loads:
        load.start()
    barrier, count = greet(reduce_peers(place) + [above, below])

    cv[pl.ds(16, 2)] = jnp.zeros((2, 64, 256), BF)
    loads[0].wait()
    loads[1].wait()
    for f in (0, 8):
        rows = flat(cv[f : f + 8])
        sum_here = rows.astype(F32)
        for k in range(3):
            sum_here = sum_here + back(flat(cv[f + k : f + k + 8]), mw[k])
        sg_rows[f : f + 8] = sum_here.astype(BF).reshape(8, 64, 256)
    pl.semaphore_wait(barrier, count)

    edges = [
        remote(video.at[:, 7], edge_in.at[0], edge_s.at[0], edge_r.at[0], below),
        remote(video.at[:, 0], edge_in.at[1], edge_s.at[1], edge_r.at[1], above),
    ]
    for copy in edges:
        copy.start()
    half_way = remote(
        sg_rows.at[pl.ds(2 * ((z + 4) % 8), 2)], sg.at[pl.ds(0, 2), z], a2a_s.at[1], a2a_r.at[4], place.along_z(4)
    )
    by_way = [
        remote(sg_rows.at[pl.ds(2 * ((z + 4) % 8), 2)], hop.at[k], hop_s.at[k], hop_r.at[k], place.along_z(d))
        for k, d in ((0, 7), (1, 1))
    ]
    onward = [
        remote(hop.at[k], sg.at[pl.ds(0, 2), (z + d) % 8], hop_s.at[2 + k], a2a_r.at[4], place.along_z(5 if k == 0 else 3))
        for k, d in ((0, 1), (1, 7))
    ]
    low = z // 4 == 0
    relays = ((z + 1) % 8 // 4 == 0, (z + 7) % 8 // 4 == 1)

    @pl.when(place.c == 0)
    def _():
        half_way.start()

    @pl.when(jnp.logical_and(place.c == 1, low))
    def _():
        by_way[0].start()

    @pl.when(jnp.logical_and(place.c == 1, jnp.logical_not(low)))
    def _():
        by_way[1].start()

    a2a = {}
    for d in (3, 5, 2, 6, 1, 7):
        peer = (z + d) % 8
        a2a[d] = remote(
            sg_rows.at[pl.ds(2 * peer, 2)], sg.at[pl.ds(0, 2), z], a2a_s.at[0], a2a_r.at[d], place.along_z(d)
        )
        a2a[d].start()
    sg[pl.ds(0, 2), z] = sg_rows[pl.ds(2 * z, 2)]

    loads[2].wait()
    loads[5].wait()
    start = valid[0]
    for f in range(4):
        values = flat(xv[f]).astype(F32)
        values = jnp.where(z * 4 + f >= start, values, 0.0)
        scale = lax.rsqrt(jnp.mean(values * values, axis=-1, keepdims=True) + 1e-06)
        normed = values * scale * gain[...]
        left, right = beside(normed)
        inverse[:, f] = scale.reshape(8, 64, 1)
        x3[1:9, f, :, 0:256] = left.astype(BF).reshape(8, 64, 256)
        x3[1:9, f, :, 256:512] = normed.astype(BF).reshape(8, 64, 256)
        x3[1:9, f, :, 512:768] = right.astype(BF).reshape(8, 64, 256)

    loads[3].wait()

    def forward(row, rows):
        cells = rows * 256
        pre = down(x3[row : row + rows].reshape(cells, 768), sw[0])
        for i in (1, 2):
            pre = pre + down(x3[row + i : row + i + rows].reshape(cells, 768), sw[i])
        q = 1.0 / (1.0 + jnp.exp(-pre))
        active[row : row + rows] = (pre * q).astype(BF).reshape(rows, 4, 64, 256)
        slope[row : row + rows] = (q * (1.0 + pre * (1.0 - q))).reshape(rows, 4, 64, 256)

    forward(1, 2)
    forward(3, 2)
    forward(5, 2)
    frame = z * 4 + lax.broadcasted_iota(jnp.int32, (256, 256), 0) // 64
    for k in (0, 1):

        @pl.when(jnp.logical_and(place.c == 1, relays[k]))
        def _():
            by_way[k].wait_recv()
            onward[k].start()

    for copy in edges:
        copy.wait()
    for side, row, inside in ((0, 0, h > 0), (1, 9, h < 15)):
        values = flat(edge_in[side]).astype(F32)
        values = jnp.where(frame >= start, values, 0.0)
        values = jnp.where(inside, values, 0.0)
        scale = lax.rsqrt(jnp.mean(values * values, axis=-1, keepdims=True) + 1e-06)
        normed = values * scale * gain[...]
        left, right = beside(normed)
        x3[row, :, :, 0:256] = left.astype(BF).reshape(4, 64, 256)
        x3[row, :, :, 256:512] = normed.astype(BF).reshape(4, 64, 256)
        x3[row, :, :, 512:768] = right.astype(BF).reshape(4, 64, 256)
    forward(0, 1)
    forward(7, 1)

    prior_copy = remote(active.at[:, 3], prior, prior_s, prior_r, place.along_z(1))

    @pl.when(z < 7)
    def _():
        prior_copy.start()


    history[pl.ds(0, 2)] = jnp.zeros((2, 64, 256), BF)
    loads[4].wait()
    st = {}

    def send_strided(s):
        for d in far:
            peer = (z + d) % 8
            st[s, d] = remote(
                strided.at[s, peer], history.at[2 + 2 * z + s], st_s, st_r, place.along_z(d)
            )
            st[s, d].start()
        history[2 + 2 * z + s] = strided[s, z]

    sum_here = down(flat(active[:, 3]), tw[0]) + down(flat(active[:, 2]), tw[1]) + down(flat(active[:, 1]), tw[2])
    strided[1] = sum_here.astype(BF).reshape(8, 64, 256)

    for i in range(3):
        for j in range(3):
            swt[i, j * 256 : (j + 1) * 256] = sw[i, j * 256 : (j + 1) * 256].T

    ahead = {}

    def send_ahead(d):
        source = (z + 8 - d) % 8
        ahead[d] = remote(sg.at[0, source], sg.at[2, source], next_s, next_r, place.along_z(7))

        @pl.when(z > 0)
        def _():
            ahead[d].start()

    send_ahead(0)
    for d in (1, 7, 2, 6, 3, 5):
        a2a[d].wait_recv()
        send_ahead(d)
    half_way.wait_recv()
    send_ahead(4)


    def pre_gradient(f, active_gradient):
        value = (active_gradient * flat(slope[:, f])).astype(BF)
        g[:, f] = value.reshape(8, 64, 256)
        left, right = beside(value.astype(F32))
        g3[1:9, f, :, 0:256] = right.astype(BF).reshape(8, 64, 256)
        g3[1:9, f, :, 256:512] = value.reshape(8, 64, 256)
        g3[1:9, f, :, 512:768] = left.astype(BF).reshape(8, 64, 256)

    sg_0, sg_1 = flat(sg[0]), flat(sg[1])
    pre_gradient(0, back(sg_0, tw[1]))
    pre_gradient(1, back(sg_0, tw[0]) + back(sg_1, tw[2]))
    pre_gradient(2, back(sg_1, tw[1]))

    for i in range(3):
        total[i * 768 : (i + 1) * 768] = outer(x3[i : i + 8, 0:3].reshape(1536, 768), g[:, 0:3].reshape(1536, 256))
    base = 9 * 256
    total[base : base + 256] = outer(flat(active[:, 1]), sg_0) + outer(flat(active[:, 3]), sg_1)
    total[base + 256 : base + 512] = outer(flat(active[:, 0]), sg_0) + outer(flat(active[:, 2]), sg_1)

    @pl.when(place.c == 0)
    def _():
        half_way.wait_send()

    @pl.when(jnp.logical_and(place.c == 1, low))
    def _():
        by_way[0].wait_send()

    @pl.when(jnp.logical_and(place.c == 1, jnp.logical_not(low)))
    def _():
        by_way[1].wait_send()

    for k in (0, 1):

        @pl.when(jnp.logical_and(place.c == 1, relays[k]))
        def _():
            onward[k].wait_send()

    @pl.when(z > 0)
    def _():
        await_bytes(sg.at[2], next_s)

    @pl.when(z < 7)
    def _():
        await_bytes(sg.at[2], next_r)

    send_strided(1)
    sg_2 = jnp.where(z < 7, flat(sg[2]).astype(F32), 0.0).astype(BF)
    pre_gradient(3, back(sg_1, tw[0]) + back(sg_2, tw[2]))
    g_edges = started(
        [
            remote(g.at[7], g_edge.at[0], ge_s.at[0], ge_r.at[0], below),
            remote(g.at[0], g_edge.at[1], ge_s.at[1], ge_r.at[1], above),
        ]
    )
    for i in range(3):
        total[i * 768 : (i + 1) * 768] += outer(x3[i : i + 8, 3].reshape(512, 768), flat(g[:, 3]))
    total[base + 512 : base + 768] = outer(flat(active[:, 1]), sg_1) + outer(flat(active[:, 3]), sg_2)
    large = DeviceSum(place, total, 0, gathered_large, sum_scratches[:18])
    small = PlaneSum(place, total, LARGE, gathered_small, sum_scratches[18:25])
    row_sum = RowSum(place, sum_scratches[25:])
    large.send_core()
    def clip_gradient(row, gain_sum):
        product = down(g3[row + 2 : row + 4].reshape(512, 768), swt[0])
        for i in (1, 2):
            product = product + down(g3[row + 2 - i : row + 4 - i].reshape(512, 768), swt[i])
        for k in range(2):
            grad = product[k * 256 : (k + 1) * 256]
            values = flat(xv[:, row + k]).astype(F32)
            values = jnp.where(frame >= start, values, 0.0)
            scale = inverse[row + k].reshape(256, 1)
            unit = values * scale
            gain_sum = gain_sum + jnp.sum(grad * unit, axis=0, keepdims=True)
            scaled = grad * gain[...]
            out = scale * (scaled - unit * jnp.mean(scaled * unit, axis=-1, keepdims=True))
            vg[:, row + k] = jnp.where(frame >= start, out, 0.0).astype(BF).reshape(4, 64, 256)
        return gain_sum

    gain_sum = jnp.zeros((1, 256), F32)
    large.send_first()
    @pl.when(z < 7)
    def _():
        prior_copy.wait_send()

    @pl.when(z > 0)
    def _():
        prior_copy.wait_recv()

    before = jnp.where(z > 0, flat(prior[...]).astype(F32), 0.0).astype(BF)
    sum_here = down(flat(active[:, 1]), tw[0]) + down(flat(active[:, 0]), tw[1]) + down(before, tw[2])
    strided[0] = sum_here.astype(BF).reshape(8, 64, 256)
    send_strided(0)
    gain_sum = clip_gradient(2, gain_sum)
    large.relay_first()
    gain_sum = clip_gradient(4, gain_sum)
    large.send_second()
    finished(g_edges)
    for side, row, inside in ((0, 0, h > 0), (1, 9, h < 15)):
        values = flat(g_edge[side]).astype(F32)
        values = jnp.where(inside, values, 0.0)
        left, right = beside(values)
        g3[row, :, :, 0:256] = right.astype(BF).reshape(4, 64, 256)
        g3[row, :, :, 256:512] = values.astype(BF).reshape(4, 64, 256)
        g3[row, :, :, 512:768] = left.astype(BF).reshape(4, 64, 256)
    gain_sum = clip_gradient(0, gain_sum)
    gain_sum = clip_gradient(6, gain_sum)
    large.start_z()
    row_sum.send(0, jnp.broadcast_to(gain_sum, (8, 256)))
    await_bytes(history.at[pl.ds(0, 14)], st_r)
    base = 12 * 256
    cot_all = flat(cv[0:16])
    for k in range(3):
        total[base + k * 256 : base + (k + 1) * 256] = outer(flat(history[2 - k : 18 - k]), cot_all)
    small.send_core()
    for f in (0, 8):
        sum_here = flat(history[f + 2 : f + 10]).astype(F32)
        for k in range(3):
            sum_here = sum_here + down(flat(history[f + 2 - k : f + 10 - k]), mw[k])
        enc[f : f + 8] = sum_here.astype(BF).reshape(8, 64, 256)
    row_sum.step(0)
    small.send_plane()
    large.start_z_back()
    row_sum.step(1)
    small.start_z()
    large.start_back()
    row_sum.step(2)
    large.back_second(0)
    large.back_first(0)
    large.back_second(1)
    small.start_back()
    large.back_first(1)
    large.back_first(3)
    large.back_first(2)
    large.back_far()
    gain_total[...] = row_sum.take(3)
    small.core_back()
    await_bytes(sg_rows.at[pl.ds(0, 12)], a2a_s.at[0])
    await_bytes(strided.at[:, pl.ds(0, 7)], st_s)
    large.finish()
    small.finish()


def finish_kernel(scale, enc, vg, large, small, gain_total, encoded, video_gradient, spatial, temporal, mix, gain_out, ws, wt, wm, wg, sems):
    copies = started(
        [
            pltpu.make_async_copy(vg, video_gradient, sems.at[0]),
            pltpu.make_async_copy(enc, encoded, sems.at[1]),
        ]
    )
    for i in range(9):
        ws[i] = large[i * 256 : (i + 1) * 256].astype(F32) * scale
        pltpu.make_async_copy(ws.at[i], spatial.at[i], sems.at[2]).start()
    for i in range(3):
        wt[i] = large[(9 + i) * 256 : (10 + i) * 256].astype(F32) * scale
    copies += started([pltpu.make_async_copy(wt, temporal, sems.at[3])])
    wm[...] = (small[...].astype(F32) * scale).reshape(3, 256, 256)
    wg[...] = gain_total[0:1] * scale
    copies += started(
        [
            pltpu.make_async_copy(wm, mix, sems.at[4]),
            pltpu.make_async_copy(wg, gain_out, sems.at[5]),
        ]
    )
    pltpu.make_async_copy(ws, spatial, sems.at[2]).wait()
    finished(copies)


def block_call(valid, gain, video, spatial_weight, temporal_weight, mix_weight, cotangent):
    vmem, dma = pltpu.VMEM, pltpu.SemaphoreType.DMA
    anywhere = pl.BlockSpec(memory_space=pltpu.HBM)
    here = pl.BlockSpec(memory_space=pltpu.VMEM)
    parts = pl.pallas_call(
        block_kernel,
        out_shape=(
            jax.ShapeDtypeStruct((16, 64, 256), BF),
            jax.ShapeDtypeStruct((4, 8, 64, 256), BF),
            jax.ShapeDtypeStruct((LARGE, 256), BF),
            jax.ShapeDtypeStruct((32, SMALL // 32, 256), BF),
            jax.ShapeDtypeStruct((8, 256), F32),
        ),
        in_specs=[pl.BlockSpec(memory_space=pltpu.SMEM)] + [anywhere] * 6,
        out_specs=(here,) * 5,
        scratch_shapes=[
            vmem((4, 8, 64, 256), BF),
            vmem((3, 768, 256), BF),
            vmem((3, 768, 256), BF),
            vmem((3, 256, 256), BF),
            vmem((3, 256, 256), BF),
            vmem((18, 64, 256), BF),
            vmem((2, 4, 64, 256), BF),
            vmem((10, 4, 64, 768), BF),
            vmem((8, 4, 64, 256), F32),
            vmem((8, 4, 64, 256), BF),
            vmem((8, 4, 64, 1), F32),
            vmem((16, 64, 256), BF),
            vmem((3, 8, 64, 256), BF),
            vmem((2, 8, 64, 256), BF),
            vmem((18, 64, 256), BF),
            vmem((8, 64, 256), BF),
            vmem((8, 4, 64, 256), BF),
            vmem((2, 4, 64, 256), BF),
            vmem((10, 4, 64, 768), BF),
            vmem((LARGE + SMALL, 256), F32),
            vmem((1, 256), F32),
            dma((6,)),
            dma((2,)),
            dma((2,)),
            dma((2,)),
            dma((8,)),
            dma,
            dma,
            dma,
            dma,
            dma,
            dma,
            dma((2,)),
            dma((2,)),
            vmem((2, 2, 64, 256), BF),
            dma((4,)),
            dma((2,)),
        ]
        + sum(sum_scratch(), []),
        compiler_params=pltpu.CompilerParams(collective_id=0, has_side_effects=True, vmem_limit_bytes=VMEM_LIMIT),
        name="down_block",
    )(
        valid,
        *[
            pltpu.with_memory_space_constraint(array, pltpu.HBM)
            for array in (gain, video, spatial_weight, temporal_weight, mix_weight, cotangent)
        ],
    )
    scale = 1.0 / math.sqrt(2 * 32 * 128 * 64)
    return pl.pallas_call(
        functools.partial(finish_kernel, scale),
        out_shape=(
            jax.ShapeDtypeStruct((16, 64, 256), BF),
            jax.ShapeDtypeStruct((4, 8, 64, 256), BF),
            jax.ShapeDtypeStruct((9, 256, 256), F32),
            jax.ShapeDtypeStruct((3, 256, 256), F32),
            jax.ShapeDtypeStruct((3, 256, 256), F32),
            jax.ShapeDtypeStruct((1, 256), F32),
        ),
        in_specs=[here] * 5,
        out_specs=(anywhere,) * 6,
        scratch_shapes=[
            vmem((9, 256, 256), F32),
            vmem((3, 256, 256), F32),
            vmem((3, 256, 256), F32),
            vmem((1, 256), F32),
            dma((6,)),
        ],
        compiler_params=pltpu.CompilerParams(vmem_limit_bytes=12 << 20),
        name="write_out",
    )(*parts)


def on_device(video_clip, valid_from, norm_gain, spatial_weight, temporal_weight, mix_weight, cotangent):
    encoded, video_gradient, spatial, temporal, mix, gain = block_call(
        valid_from,
        norm_gain.reshape(1, 256),
        video_clip.reshape(4, 8, 64, 256),
        spatial_weight.reshape(3, 768, 256),
        temporal_weight,
        mix_weight,
        cotangent.reshape(16, 64, 256),
    )
    return (
        encoded.reshape(1, 16, 1, 64, 256),
        video_gradient.reshape(1, 4, 8, 64, 256),
        spatial.reshape(3, 3, 256, 256),
        temporal,
        mix,
        gain.reshape(256),
    )


def solution(mesh):
    return jax.shard_map(
        on_device,
        mesh=mesh,
        in_specs=(
            P("cam", "tm", "height", None, None),
            P("cam"),
            P(),
            P(),
            P(),
            P(),
            P("cam", None, ("height", "tm"), None, None),
        ),
        out_specs=(
            P("cam", None, ("height", "tm"), None, None),
            P("cam", "tm", "height", None, None),
            P(),
            P(),
            P(),
            P(),
        ),
        check_vma=False,
    )
```

```python
import functools
import math

import jax
import jax.numpy as jnp
from jax import lax
from jax.experimental import pallas as pl
from jax.experimental.pallas import tpu as pltpu
from jax.sharding import PartitionSpec as P

MESH = pl.DeviceIdType.MESH
BF = jnp.bfloat16
F32 = jnp.float32
LARGE = 12 * 256
SMALL = 3 * 256
VMEM_LIMIT = 46 << 20


class Place:
    def __init__(self):
        self.z = lax.axis_index("tm")
        self.h = lax.axis_index("height")
        self.c = lax.axis_index("cam")
        self.x = self.h // 4
        self.y = self.h % 4
        self.first = (1 - self.c) * self.x + self.c * self.y
        self.second = (1 - self.c) * self.y + self.c * self.x

    def across(self):
        return {"cam": 1 - self.c}

    def along_first(self, d):
        other = (self.first + d) % 4
        return {"height": (1 - self.c) * (other * 4 + self.y) + self.c * (self.x * 4 + other)}

    def along_second(self, d):
        other = (self.second + d) % 4
        return {"height": (1 - self.c) * (self.x * 4 + other) + self.c * (other * 4 + self.y)}

    def along_x(self, d):
        return {"height": (self.x + d) % 4 * 4 + self.y}

    def along_y(self, d):
        return {"height": self.x * 4 + (self.y + d) % 4}

    def in_plane(self, d):
        return {"height": (self.h + d) % 16}

    def along_z(self, d):
        return {"tm": (self.z + d) % 8}


def remote(src, dst, send, recv, where):
    return pltpu.make_async_remote_copy(
        src_ref=src, dst_ref=dst, send_sem=send, recv_sem=recv, device_id=where, device_id_type=MESH
    )


def greet(peers):
    barrier = pltpu.get_barrier_semaphore()
    for peer in peers:
        pl.semaphore_signal(barrier, inc=1, device_id=peer, device_id_type=MESH)
    return barrier, len(peers)


def reduce_peers(place):
    return [place.across()] + [place.in_plane(d) for d in range(1, 16)] + [place.along_z(d) for d in range(1, 8)]


def block(ref, start, rows):
    return ref.at[pl.ds(pl.multiple_of(start, 16), rows)]


def started(copies):
    for copy in copies:
        copy.start()
    return copies


def finished(copies):
    for copy in copies:
        copy.wait()


ORDER = (2, 1, 3, 0)
UP = (2, 1)
BACK_ORDER = (0, 1, 3, 2)
FAR_FIRST = (4, 3, 5, 2, 6, 1, 7)
PLANE = (10, 5, 15, 7, 13, 9, 11, 6, 14, 8, 2, 12, 4, 3, 1)


def await_bytes(ref, sem):
    pltpu.make_async_copy(ref, ref, sem).wait()


def kind_of(group, e):
    return (2, 3 if e in UP else 1, 1 if e in UP else 3, 0)[group]


class DeviceSum:
    def __init__(self, place, total, base, gathered, scratch):
        self.place, self.total, self.base, self.gathered = place, total, base, gathered
        (
            self.halved,
            self.landed_c,
            self.held_1,
            self.landed_1,
            self.held_2,
            self.landed_2,
            self.own_2,
            self.held_3,
            self.landed_3,
            self.placed_3,
            self.sent,
            self.core_r,
            self.first_r,
            self.second_r,
            self.z_r,
            self.second_back_r,
            self.first_back_r,
            self.core_back_r,
        ) = scratch
        rows = gathered.shape[0]
        self.half, self.n1, self.n2, self.n3 = rows // 2, rows // 8, rows // 32, rows // 256
        self.mine = place.c * self.half

    def rows(self, start):
        return pl.ds(pl.multiple_of(start, 16), self.n2)

    def piece(self, d, e):
        place = self.place
        return self.mine + (place.first + d) % 4 * self.n1 + (place.second + e) % 4 * self.n2

    def send_core(self):
        place = self.place
        other = self.base + (1 - place.c) * self.half
        for group in range(4):
            for i, e in enumerate(ORDER):
                d = kind_of(group, e)
                at = other + (place.second + d) % 4 * self.n1 + (place.first + e) % 4 * self.n2
                self.halved[group * 4 + i] = self.total[self.rows(at), :].astype(BF)
        for group in range(4):
            four = pl.ds(group * 4, 4)
            remote(
                self.halved.at[four], self.landed_c.at[four], self.sent.at[0], self.core_r.at[group], place.across()
            ).start()

    def await_core(self, group):
        await_bytes(self.landed_c.at[pl.ds(group * 4, 4)], self.core_r.at[group])

    def chip_sum(self, group, i, e):
        at = self.base + self.piece(kind_of(group, e), e)
        return self.total[self.rows(at), :] + self.landed_c[group * 4 + i].astype(F32)

    def send_held(self, group, i, value, d):
        k = group * 4 + i
        self.held_1[k] = value.astype(BF)
        remote(
            self.held_1.at[k],
            self.landed_1.at[k],
            self.sent.at[1],
            self.first_r.at[group],
            self.place.along_first(d),
        ).start()

    def send_first(self):
        self.await_core(0)
        for i, e in enumerate(ORDER):
            self.send_held(0, i, self.chip_sum(0, i, e), 1 if e in UP else 3)
        self.await_core(1)
        for i, e in enumerate(ORDER):
            self.send_held(1, i, self.chip_sum(1, i, e), kind_of(1, e))

    def relay_first(self):
        self.await_core(2)
        await_bytes(self.landed_1.at[pl.ds(0, 4)], self.first_r.at[0])
        for i, e in enumerate(ORDER):
            self.send_held(2, i, self.chip_sum(2, i, e) + self.landed_1[i].astype(F32), kind_of(2, e))

    def send_second(self):
        self.await_core(3)
        for group in (1, 2):
            await_bytes(self.landed_1.at[pl.ds(group * 4, 4)], self.first_r.at[group])
        for i, e in enumerate(ORDER):
            sum_here = self.chip_sum(3, i, e)
            sum_here = sum_here + self.landed_1[4 + i].astype(F32) + self.landed_1[8 + i].astype(F32)
            if e == 0:
                self.own_2[...] = sum_here
                continue
            self.held_2[e - 1] = sum_here.astype(BF)
            remote(
                self.held_2.at[e - 1],
                self.landed_2.at[e - 1],
                self.sent.at[2],
                self.second_r,
                self.place.along_second(e),
            ).start()

    def start_z(self):
        await_bytes(self.landed_2, self.second_r)
        sum_here = self.own_2[...]
        for e in (1, 2, 3):
            sum_here = sum_here + self.landed_2[e - 1].astype(F32)
        for k in range(8):
            self.held_3[k, 0 : self.n3] = sum_here[k * self.n3 : (k + 1) * self.n3].astype(BF)
        for d in FAR_FIRST:
            remote(
                self.held_3.at[(self.place.z + d) % 8],
                self.landed_3.at[d - 1],
                self.sent.at[3],
                self.z_r.at[0],
                self.place.along_z(d),
            ).start()

    def start_z_back(self):
        await_bytes(self.landed_3, self.z_r.at[0])
        z = self.place.z
        sum_here = self.held_3[z].astype(F32)
        for d in range(1, 8):
            sum_here = sum_here + self.landed_3[d - 1].astype(F32)
        self.placed_3[z] = sum_here.astype(BF)
        for d in FAR_FIRST:
            remote(
                self.placed_3.at[z], self.placed_3.at[z], self.sent.at[4], self.z_r.at[1], self.place.along_z(d)
            ).start()

    def start_back(self):
        await_bytes(self.landed_3, self.z_r.at[1])
        pieces = [self.placed_3[k].astype(F32)[0 : self.n3] for k in range(8)]
        self.gathered[self.rows(self.piece(0, 0)), :] = jnp.concatenate(pieces).astype(BF)
        for d in (2, 1, 3):
            self.copy_back(self.piece(0, 0), 5, self.second_back_r.at[d // 2 if d == 2 else 0], self.place.along_second(d))
        self.hand_on(0)

    def copy_back(self, start, sent, received, where):
        at = self.gathered.at[self.rows(start)]
        remote(at, at, self.sent.at[sent], received, where).start()

    def hand_on(self, e):
        for d in (1, 3):
            self.copy_back(self.piece(0, 4 - e), 6, self.first_back_r.at[e], self.place.along_first(d))
        self.copy_back(self.piece(0, 4 - e), 7, self.core_back_r, self.place.across())

    def back_second(self, which):
        await_bytes(self.landed_2.at[pl.ds(0, 2 - which)], self.second_back_r.at[which])
        for e in ((1, 3), (2,))[which]:
            self.hand_on(e)

    def back_first(self, e):
        await_bytes(self.landed_1.at[pl.ds(0, 2)], self.first_back_r.at[e])
        for d in (1, 3):
            at = self.piece(4 - d, 4 - e)
            if d == (1 if e in UP else 3):
                self.copy_back(at, 6, self.first_back_r.at[4], self.place.along_first(d))
            self.copy_back(at, 7, self.core_back_r, self.place.across())

    def back_far(self):
        await_bytes(self.landed_1.at[pl.ds(0, 4)], self.first_back_r.at[4])
        for e in BACK_ORDER:
            self.copy_back(self.piece(2, 4 - e), 7, self.core_back_r, self.place.across())

    def finish(self):
        await_bytes(self.landed_c, self.core_back_r)
        for k, ref in enumerate(
            (
                self.halved,
                self.held_1,
                self.held_2,
                self.landed_3,
                self.landed_3,
                self.held_2,
                self.held_1,
                self.halved,
            )
        ):
            await_bytes(ref, self.sent.at[k])


class PlaneSum:
    def __init__(self, place, total, base, gathered, scratch):
        self.place, self.total, self.base, self.gathered = place, total, base, gathered
        self.halved, self.landed_c, self.held, self.landed, self.landed_z, self.sent, self.received = scratch
        self.n = gathered.shape[1]
        self.half = 16 * self.n
        self.mine = place.c * self.half

    def send_core(self):
        other = pl.multiple_of(self.base + (1 - self.place.c) * self.half, 16)
        self.halved[...] = self.total[pl.ds(other, self.half), :].reshape(16, self.n, 256).astype(BF)
        remote(self.halved, self.landed_c, self.sent.at[0], self.received.at[0], self.place.across()).start()

    def send_plane(self):
        await_bytes(self.landed_c, self.received.at[0])
        own = pl.multiple_of(self.base + self.mine, 16)
        value = self.total[pl.ds(own, self.half), :].reshape(16, self.n, 256) + self.landed_c[...].astype(F32)
        self.held[...] = value.astype(BF)
        for d in PLANE:
            remote(
                self.held.at[(self.place.h + d) % 16],
                self.landed.at[d - 1],
                self.sent.at[1],
                self.received.at[1],
                self.place.in_plane(d),
            ).start()

    def start_z(self):
        await_bytes(self.landed, self.received.at[1])
        sum_here = self.held[self.place.h].astype(F32)
        for k in range(15):
            sum_here = sum_here + self.landed[k].astype(F32)
        z = self.place.z
        self.landed_z[z] = sum_here.astype(BF)
        for d in FAR_FIRST:
            remote(
                self.landed_z.at[z], self.landed_z.at[z], self.sent.at[2], self.received.at[2], self.place.along_z(d)
            ).start()

    def start_back(self):
        await_bytes(self.landed_z.at[pl.ds(0, 7)], self.received.at[2])
        sum_here = self.landed_z[0].astype(F32)
        for k in range(1, 8):
            sum_here = sum_here + self.landed_z[k].astype(F32)
        mine = self.place.c * 16 + self.place.h
        self.gathered[mine] = sum_here.astype(BF)
        at = self.gathered.at[mine]
        for d in PLANE:
            remote(at, at, self.sent.at[3], self.received.at[3], self.place.in_plane(d)).start()

    def core_back(self):
        await_bytes(self.landed, self.received.at[3])
        at = self.gathered.at[pl.ds(self.place.c * 16, 16)]
        remote(at, at, self.sent.at[4], self.received.at[4], self.place.across()).start()

    def finish(self):
        await_bytes(self.landed_c, self.received.at[4])
        for k, ref in enumerate((self.halved, self.landed, self.landed_z.at[pl.ds(0, 7)], self.landed, self.halved)):
            await_bytes(ref, self.sent.at[k])


class RowSum:
    def __init__(self, place, scratch):
        self.place = place
        self.slots, self.sent, self.received = scratch[:4], scratch[4], scratch[5]
        self.at = (place.c, place.x, place.y, place.z)
        self.peers = (
            [place.across()],
            [place.along_x(d) for d in (1, 2, 3)],
            [place.along_y(d) for d in (1, 2, 3)],
            [place.along_z(d) for d in range(1, 8)],
        )

    def send(self, stage, value):
        slots, at = self.slots[stage], self.at[stage]
        slots[at] = value
        for peer in self.peers[stage]:
            remote(slots.at[at], slots.at[at], self.sent.at[stage], self.received.at[stage], peer).start()

    def take(self, stage):
        slots = self.slots[stage]
        others = slots.at[pl.ds(0, slots.shape[0] - 1)]
        await_bytes(others, self.received.at[stage])
        await_bytes(others, self.sent.at[stage])
        value = slots[0]
        for k in range(1, slots.shape[0]):
            value = value + slots[k]
        return value

    def step(self, stage):
        self.send(stage + 1, self.take(stage))


def sum_scratch():
    dma, vmem = pltpu.SemaphoreType.DMA, pltpu.VMEM
    n2, n = LARGE // 32, SMALL // 32
    large = [
        vmem((16, n2, 256), BF),
        vmem((16, n2, 256), BF),
        vmem((12, n2, 256), BF),
        vmem((12, n2, 256), BF),
        vmem((3, n2, 256), BF),
        vmem((3, n2, 256), BF),
        vmem((n2, 256), F32),
        vmem((8, 16, 256), BF),
        vmem((7, 16, 256), BF),
        vmem((8, 16, 256), BF),
        dma((8,)),
        dma((4,)),
        dma((3,)),
        dma,
        dma((2,)),
        dma((2,)),
        dma((5,)),
        dma,
    ]
    small = [
        vmem((16, n, 256), BF),
        vmem((16, n, 256), BF),
        vmem((16, n, 256), BF),
        vmem((15, n, 256), BF),
        vmem((8, n, 256), BF),
        dma((5,)),
        dma((5,)),
    ]
    row = [vmem((k, 8, 256), F32) for k in (2, 4, 4, 8)] + [dma((4,)), dma((4,))]
    return large, small, row


def down(left, right):
    return lax.dot_general(left, right, (((1,), (0,)), ((), ())), preferred_element_type=F32)


def back(left, right):
    return lax.dot_general(left, right, (((1,), (1,)), ((), ())), preferred_element_type=F32)


def outer(left, right):
    return lax.dot_general(left, right, (((0,), (0,)), ((), ())), preferred_element_type=F32)


def flat(value):
    return value.reshape(-1, value.shape[-1])


def beside(rows):
    cells = rows.shape[0]
    column = lax.broadcasted_iota(jnp.int32, (cells, 256), 0) % 64
    left = jnp.where(column == 0, 0.0, pltpu.roll(rows, 1, 0))
    right = jnp.where(column == 63, 0.0, pltpu.roll(rows, cells - 1, 0))
    return left, right


def block_kernel(
    valid,
    gain_from,
    video,
    spatial_weight,
    temporal_weight,
    mix_weight,
    cotangent,
    enc,
    vg,
    gathered_large,
    gathered_small,
    gain_total,
    xv,
    sw,
    swt,
    tw,
    mw,
    cv,
    edge_in,
    x3,
    slope,
    active,
    inverse,
    sg_rows,
    sg,
    strided,
    history,
    prior,
    g,
    g_edge,
    g3,
    total,
    gain,
    load_sems,
    edge_s,
    edge_r,
    a2a_s,
    a2a_r,
    next_s,
    next_r,
    prior_s,
    prior_r,
    st_s,
    st_r,
    ge_s,
    ge_r,
    hop,
    hop_s,
    hop_r,
    *sum_scratches,
):
    place = Place()
    z, h = place.z, place.h
    above, below = {"height": (h + 15) % 16}, {"height": (h + 1) % 16}
    far = (4, 3, 5, 2, 6, 1, 7)

    loads = [
        pltpu.make_async_copy(cotangent, cv.at[pl.ds(0, 16)], load_sems.at[0]),
        pltpu.make_async_copy(mix_weight, mw, load_sems.at[1]),
        pltpu.make_async_copy(video, xv, load_sems.at[2]),
        pltpu.make_async_copy(spatial_weight, sw, load_sems.at[3]),
        pltpu.make_async_copy(temporal_weight, tw, load_sems.at[4]),
        pltpu.make_async_copy(gain_from, gain, load_sems.at[5]),
    ]
    for load in loads:
        load.start()
    barrier, count = greet(reduce_peers(place) + [above, below])

    cv[pl.ds(16, 2)] = jnp.zeros((2, 64, 256), BF)
    loads[0].wait()
    loads[1].wait()
    for f in (0, 8):
        rows = flat(cv[f : f + 8])
        sum_here = rows.astype(F32)
        for k in range(3):
            sum_here = sum_here + back(flat(cv[f + k : f + k + 8]), mw[k])
        sg_rows[f : f + 8] = sum_here.astype(BF).reshape(8, 64, 256)
    pl.semaphore_wait(barrier, count)

    edges = [
        remote(video.at[:, 7], edge_in.at[0], edge_s.at[0], edge_r.at[0], below),
        remote(video.at[:, 0], edge_in.at[1], edge_s.at[1], edge_r.at[1], above),
    ]
    for copy in edges:
        copy.start()
    half_way = remote(
        sg_rows.at[pl.ds(2 * ((z + 4) % 8), 2)], sg.at[pl.ds(0, 2), z], a2a_s.at[1], a2a_r.at[4], place.along_z(4)
    )
    by_way = [
        remote(sg_rows.at[pl.ds(2 * ((z + 4) % 8), 2)], hop.at[k], hop_s.at[k], hop_r.at[k], place.along_z(d))
        for k, d in ((0, 7), (1, 1))
    ]
    onward = [
        remote(hop.at[k], sg.at[pl.ds(0, 2), (z + d) % 8], hop_s.at[2 + k], a2a_r.at[4], place.along_z(5 if k == 0 else 3))
        for k, d in ((0, 1), (1, 7))
    ]
    low = z // 4 == 0
    relays = ((z + 1) % 8 // 4 == 0, (z + 7) % 8 // 4 == 1)

    @pl.when(place.c == 0)
    def _():
        half_way.start()

    @pl.when(jnp.logical_and(place.c == 1, low))
    def _():
        by_way[0].start()

    @pl.when(jnp.logical_and(place.c == 1, jnp.logical_not(low)))
    def _():
        by_way[1].start()

    a2a = {}
    for d in (3, 5, 2, 6, 1, 7):
        peer = (z + d) % 8
        a2a[d] = remote(
            sg_rows.at[pl.ds(2 * peer, 2)], sg.at[pl.ds(0, 2), z], a2a_s.at[0], a2a_r.at[d], place.along_z(d)
        )
        a2a[d].start()
    sg[pl.ds(0, 2), z] = sg_rows[pl.ds(2 * z, 2)]

    loads[2].wait()
    loads[5].wait()
    start = valid[0]
    for f in range(4):
        values = flat(xv[f]).astype(F32)
        values = jnp.where(z * 4 + f >= start, values, 0.0)
        scale = lax.rsqrt(jnp.mean(values * values, axis=-1, keepdims=True) + 1e-06)
        normed = values * scale * gain[...]
        left, right = beside(normed)
        inverse[:, f] = scale.reshape(8, 64, 1)
        x3[1:9, f, :, 0:256] = left.astype(BF).reshape(8, 64, 256)
        x3[1:9, f, :, 256:512] = normed.astype(BF).reshape(8, 64, 256)
        x3[1:9, f, :, 512:768] = right.astype(BF).reshape(8, 64, 256)

    loads[3].wait()

    def forward(row, rows):
        cells = rows * 256
        pre = down(x3[row : row + rows].reshape(cells, 768), sw[0])
        for i in (1, 2):
            pre = pre + down(x3[row + i : row + i + rows].reshape(cells, 768), sw[i])
        q = 1.0 / (1.0 + jnp.exp(-pre))
        active[row : row + rows] = (pre * q).astype(BF).reshape(rows, 4, 64, 256)
        slope[row : row + rows] = (q * (1.0 + pre * (1.0 - q))).reshape(rows, 4, 64, 256)

    forward(1, 2)
    forward(3, 2)
    forward(5, 2)
    frame = z * 4 + lax.broadcasted_iota(jnp.int32, (256, 256), 0) // 64
    for k in (0, 1):

        @pl.when(jnp.logical_and(place.c == 1, relays[k]))
        def _():
            by_way[k].wait_recv()
            onward[k].start()

    for copy in edges:
        copy.wait()
    for side, row, inside in ((0, 0, h > 0), (1, 9, h < 15)):
        values = flat(edge_in[side]).astype(F32)
        values = jnp.where(frame >= start, values, 0.0)
        values = jnp.where(inside, values, 0.0)
        scale = lax.rsqrt(jnp.mean(values * values, axis=-1, keepdims=True) + 1e-06)
        normed = values * scale * gain[...]
        left, right = beside(normed)
        x3[row, :, :, 0:256] = left.astype(BF).reshape(4, 64, 256)
        x3[row, :, :, 256:512] = normed.astype(BF).reshape(4, 64, 256)
        x3[row, :, :, 512:768] = right.astype(BF).reshape(4, 64, 256)
    forward(0, 1)
    forward(7, 1)

    prior_copy = remote(active.at[:, 3], prior, prior_s, prior_r, place.along_z(1))


    history[pl.ds(0, 2)] = jnp.zeros((2, 64, 256), BF)
    loads[4].wait()
    st = {}

    def send_strided(s):
        for d in far:
            peer = (z + d) % 8
            st[s, d] = remote(
                strided.at[s, peer], history.at[2 + 2 * z + s], st_s, st_r, place.along_z(d)
            )
            st[s, d].start()
        history[2 + 2 * z + s] = strided[s, z]

    sum_here = down(flat(active[:, 3]), tw[0]) + down(flat(active[:, 2]), tw[1]) + down(flat(active[:, 1]), tw[2])
    strided[1] = sum_here.astype(BF).reshape(8, 64, 256)

    for i in range(3):
        for j in range(3):
            swt[i, j * 256 : (j + 1) * 256] = sw[i, j * 256 : (j + 1) * 256].T

    ahead = {}

    def send_ahead(d):
        source = (z + 8 - d) % 8
        ahead[d] = remote(sg.at[0, source], sg.at[2, source], next_s, next_r, place.along_z(7))

        @pl.when(z > 0)
        def _():
            ahead[d].start()

    send_ahead(0)
    for d in (1, 7, 2, 6):
        a2a[d].wait_recv()
        send_ahead(d)

    @pl.when(z < 7)
    def _():
        prior_copy.start()

    for d in (3, 5):
        a2a[d].wait_recv()
        send_ahead(d)
    half_way.wait_recv()
    send_ahead(4)


    def pre_gradient(f, active_gradient):
        value = (active_gradient * flat(slope[:, f])).astype(BF)
        g[:, f] = value.reshape(8, 64, 256)
        left, right = beside(value.astype(F32))
        g3[1:9, f, :, 0:256] = right.astype(BF).reshape(8, 64, 256)
        g3[1:9, f, :, 256:512] = value.reshape(8, 64, 256)
        g3[1:9, f, :, 512:768] = left.astype(BF).reshape(8, 64, 256)

    sg_0, sg_1 = flat(sg[0]), flat(sg[1])
    pre_gradient(0, back(sg_0, tw[1]))
    pre_gradient(1, back(sg_0, tw[0]) + back(sg_1, tw[2]))
    pre_gradient(2, back(sg_1, tw[1]))

    for i in range(3):
        total[i * 768 : (i + 1) * 768] = outer(x3[i : i + 8, 0:3].reshape(1536, 768), g[:, 0:3].reshape(1536, 256))
    base = 9 * 256
    total[base : base + 256] = outer(flat(active[:, 1]), sg_0) + outer(flat(active[:, 3]), sg_1)
    total[base + 256 : base + 512] = outer(flat(active[:, 0]), sg_0) + outer(flat(active[:, 2]), sg_1)

    @pl.when(place.c == 0)
    def _():
        half_way.wait_send()

    @pl.when(jnp.logical_and(place.c == 1, low))
    def _():
        by_way[0].wait_send()

    @pl.when(jnp.logical_and(place.c == 1, jnp.logical_not(low)))
    def _():
        by_way[1].wait_send()

    for k in (0, 1):

        @pl.when(jnp.logical_and(place.c == 1, relays[k]))
        def _():
            onward[k].wait_send()

    @pl.when(z > 0)
    def _():
        await_bytes(sg.at[2], next_s)

    @pl.when(z < 7)
    def _():
        await_bytes(sg.at[2], next_r)

    sg_2 = jnp.where(z < 7, flat(sg[2]).astype(F32), 0.0).astype(BF)
    pre_gradient(3, back(sg_1, tw[0]) + back(sg_2, tw[2]))
    g_edges = started(
        [
            remote(g.at[7], g_edge.at[0], ge_s.at[0], ge_r.at[0], below),
            remote(g.at[0], g_edge.at[1], ge_s.at[1], ge_r.at[1], above),
        ]
    )
    for i in range(3):
        total[i * 768 : (i + 1) * 768] += outer(x3[i : i + 8, 3].reshape(512, 768), flat(g[:, 3]))
    total[base + 512 : base + 768] = outer(flat(active[:, 1]), sg_1) + outer(flat(active[:, 3]), sg_2)
    large = DeviceSum(place, total, 0, gathered_large, sum_scratches[:18])
    small = PlaneSum(place, total, LARGE, gathered_small, sum_scratches[18:25])
    row_sum = RowSum(place, sum_scratches[25:])
    large.send_core()
    send_strided(1)
    def clip_gradient(row, gain_sum):
        product = down(g3[row + 2 : row + 4].reshape(512, 768), swt[0])
        for i in (1, 2):
            product = product + down(g3[row + 2 - i : row + 4 - i].reshape(512, 768), swt[i])
        for k in range(2):
            grad = product[k * 256 : (k + 1) * 256]
            values = flat(xv[:, row + k]).astype(F32)
            values = jnp.where(frame >= start, values, 0.0)
            scale = inverse[row + k].reshape(256, 1)
            unit = values * scale
            gain_sum = gain_sum + jnp.sum(grad * unit, axis=0, keepdims=True)
            scaled = grad * gain[...]
            out = scale * (scaled - unit * jnp.mean(scaled * unit, axis=-1, keepdims=True))
            vg[:, row + k] = jnp.where(frame >= start, out, 0.0).astype(BF).reshape(4, 64, 256)
        return gain_sum

    gain_sum = jnp.zeros((1, 256), F32)
    large.send_first()
    @pl.when(z < 7)
    def _():
        prior_copy.wait_send()

    @pl.when(z > 0)
    def _():
        prior_copy.wait_recv()

    before = jnp.where(z > 0, flat(prior[...]).astype(F32), 0.0).astype(BF)
    sum_here = down(flat(active[:, 1]), tw[0]) + down(flat(active[:, 0]), tw[1]) + down(before, tw[2])
    strided[0] = sum_here.astype(BF).reshape(8, 64, 256)
    send_strided(0)
    gain_sum = clip_gradient(2, gain_sum)
    large.relay_first()
    gain_sum = clip_gradient(4, gain_sum)
    large.send_second()
    finished(g_edges)
    for side, row, inside in ((0, 0, h > 0), (1, 9, h < 15)):
        values = flat(g_edge[side]).astype(F32)
        values = jnp.where(inside, values, 0.0)
        left, right = beside(values)
        g3[row, :, :, 0:256] = right.astype(BF).reshape(4, 64, 256)
        g3[row, :, :, 256:512] = values.astype(BF).reshape(4, 64, 256)
        g3[row, :, :, 512:768] = left.astype(BF).reshape(4, 64, 256)
    gain_sum = clip_gradient(0, gain_sum)
    gain_sum = clip_gradient(6, gain_sum)
    large.start_z()
    row_sum.send(0, jnp.broadcast_to(gain_sum, (8, 256)))
    await_bytes(history.at[pl.ds(0, 14)], st_r)
    base = 12 * 256
    cot_all = flat(cv[0:16])
    for k in range(3):
        total[base + k * 256 : base + (k + 1) * 256] = outer(flat(history[2 - k : 18 - k]), cot_all)
    small.send_core()
    for f in (0, 8):
        sum_here = flat(history[f + 2 : f + 10]).astype(F32)
        for k in range(3):
            sum_here = sum_here + down(flat(history[f + 2 - k : f + 10 - k]), mw[k])
        enc[f : f + 8] = sum_here.astype(BF).reshape(8, 64, 256)
    row_sum.step(0)
    small.send_plane()
    large.start_z_back()
    row_sum.step(1)
    small.start_z()
    large.start_back()
    row_sum.step(2)
    large.back_first(0)
    large.back_second(0)
    large.back_second(1)
    small.start_back()
    large.back_first(1)
    large.back_first(3)
    large.back_first(2)
    large.back_far()
    gain_total[...] = row_sum.take(3)
    small.core_back()
    await_bytes(sg_rows.at[pl.ds(0, 12)], a2a_s.at[0])
    await_bytes(strided.at[:, pl.ds(0, 7)], st_s)
    large.finish()
    small.finish()


def finish_kernel(scale, enc, vg, large, small, gain_total, encoded, video_gradient, spatial, temporal, mix, gain_out, ws, wt, wm, wg, sems):
    copies = started(
        [
            pltpu.make_async_copy(vg, video_gradient, sems.at[0]),
            pltpu.make_async_copy(enc, encoded, sems.at[1]),
        ]
    )
    for i in range(9):
        ws[i] = large[i * 256 : (i + 1) * 256].astype(F32) * scale
        pltpu.make_async_copy(ws.at[i], spatial.at[i], sems.at[2]).start()
    for i in range(3):
        wt[i] = large[(9 + i) * 256 : (10 + i) * 256].astype(F32) * scale
    copies += started([pltpu.make_async_copy(wt, temporal, sems.at[3])])
    wm[...] = (small[...].astype(F32) * scale).reshape(3, 256, 256)
    wg[...] = gain_total[0:1] * scale
    copies += started(
        [
            pltpu.make_async_copy(wm, mix, sems.at[4]),
            pltpu.make_async_copy(wg, gain_out, sems.at[5]),
        ]
    )
    pltpu.make_async_copy(ws, spatial, sems.at[2]).wait()
    finished(copies)


def block_call(valid, gain, video, spatial_weight, temporal_weight, mix_weight, cotangent):
    vmem, dma = pltpu.VMEM, pltpu.SemaphoreType.DMA
    anywhere = pl.BlockSpec(memory_space=pltpu.HBM)
    here = pl.BlockSpec(memory_space=pltpu.VMEM)
    parts = pl.pallas_call(
        block_kernel,
        out_shape=(
            jax.ShapeDtypeStruct((16, 64, 256), BF),
            jax.ShapeDtypeStruct((4, 8, 64, 256), BF),
            jax.ShapeDtypeStruct((LARGE, 256), BF),
            jax.ShapeDtypeStruct((32, SMALL // 32, 256), BF),
            jax.ShapeDtypeStruct((8, 256), F32),
        ),
        in_specs=[pl.BlockSpec(memory_space=pltpu.SMEM)] + [anywhere] * 6,
        out_specs=(here,) * 5,
        scratch_shapes=[
            vmem((4, 8, 64, 256), BF),
            vmem((3, 768, 256), BF),
            vmem((3, 768, 256), BF),
            vmem((3, 256, 256), BF),
            vmem((3, 256, 256), BF),
            vmem((18, 64, 256), BF),
            vmem((2, 4, 64, 256), BF),
            vmem((10, 4, 64, 768), BF),
            vmem((8, 4, 64, 256), F32),
            vmem((8, 4, 64, 256), BF),
            vmem((8, 4, 64, 1), F32),
            vmem((16, 64, 256), BF),
            vmem((3, 8, 64, 256), BF),
            vmem((2, 8, 64, 256), BF),
            vmem((18, 64, 256), BF),
            vmem((8, 64, 256), BF),
            vmem((8, 4, 64, 256), BF),
            vmem((2, 4, 64, 256), BF),
            vmem((10, 4, 64, 768), BF),
            vmem((LARGE + SMALL, 256), F32),
            vmem((1, 256), F32),
            dma((6,)),
            dma((2,)),
            dma((2,)),
            dma((2,)),
            dma((8,)),
            dma,
            dma,
            dma,
            dma,
            dma,
            dma,
            dma((2,)),
            dma((2,)),
            vmem((2, 2, 64, 256), BF),
            dma((4,)),
            dma((2,)),
        ]
        + sum(sum_scratch(), []),
        compiler_params=pltpu.CompilerParams(collective_id=0, has_side_effects=True, vmem_limit_bytes=VMEM_LIMIT),
        name="down_block",
    )(
        valid,
        *[
            pltpu.with_memory_space_constraint(array, pltpu.HBM)
            for array in (gain, video, spatial_weight, temporal_weight, mix_weight, cotangent)
        ],
    )
    scale = 1.0 / math.sqrt(2 * 32 * 128 * 64)
    return pl.pallas_call(
        functools.partial(finish_kernel, scale),
        out_shape=(
            jax.ShapeDtypeStruct((16, 64, 256), BF),
            jax.ShapeDtypeStruct((4, 8, 64, 256), BF),
            jax.ShapeDtypeStruct((9, 256, 256), F32),
            jax.ShapeDtypeStruct((3, 256, 256), F32),
            jax.ShapeDtypeStruct((3, 256, 256), F32),
            jax.ShapeDtypeStruct((1, 256), F32),
        ),
        in_specs=[here] * 5,
        out_specs=(anywhere,) * 6,
        scratch_shapes=[
            vmem((9, 256, 256), F32),
            vmem((3, 256, 256), F32),
            vmem((3, 256, 256), F32),
            vmem((1, 256), F32),
            dma((6,)),
        ],
        compiler_params=pltpu.CompilerParams(vmem_limit_bytes=12 << 20),
        name="write_out",
    )(*parts)


def on_device(video_clip, valid_from, norm_gain, spatial_weight, temporal_weight, mix_weight, cotangent):
    encoded, video_gradient, spatial, temporal, mix, gain = block_call(
        valid_from,
        norm_gain.reshape(1, 256),
        video_clip.reshape(4, 8, 64, 256),
        spatial_weight.reshape(3, 768, 256),
        temporal_weight,
        mix_weight,
        cotangent.reshape(16, 64, 256),
    )
    return (
        encoded.reshape(1, 16, 1, 64, 256),
        video_gradient.reshape(1, 4, 8, 64, 256),
        spatial.reshape(3, 3, 256, 256),
        temporal,
        mix,
        gain.reshape(256),
    )


def solution(mesh):
    return jax.shard_map(
        on_device,
        mesh=mesh,
        in_specs=(
            P("cam", "tm", "height", None, None),
            P("cam"),
            P(),
            P(),
            P(),
            P(),
            P("cam", None, ("height", "tm"), None, None),
        ),
        out_specs=(
            P("cam", None, ("height", "tm"), None, None),
            P("cam", "tm", "height", None, None),
            P(),
            P(),
            P(),
            P(),
        ),
        check_vma=False,
    )
```
